32 devices in a mesh: dp: 8 (over y, x, core), tensor: 4 (over z).
Axes of the slice: x: 2, y: 2, z: 4, core: 2. Of those that a mesh axis runs over, the one named last changes fastest.
Arguments:
- block_in: float32 [4096, 1152], P(('dp', 'tensor')), may hold values from -6 to 6
- out_grad: float32 [4096, 1152], P(('dp', 'tensor')), may hold values from -6 to 6
- segments: int32 [4096], replicated, may hold values from 0 to 7, never falling along the last dimension, each value on 1 to 3072 neighbouring positions
- w_query: bfloat16 [1152, 1024], P('dp', 'tensor'), may hold values from -0.1875 to 0.1875
- w_keyval: bfloat16 [1152, 512], P(('dp', 'tensor')), may hold values from -0.1875 to 0.1875
- w_out: bfloat16 [1024, 1152], P('tensor', 'dp'), may hold values from -0.1875 to 0.1875
- w_gate: bfloat16 [1152, 6912], P('dp', 'tensor'), may hold values from -0.1875 to 0.1875
- w_up: bfloat16 [1152, 6912], P('dp', 'tensor'), may hold values from -0.1875 to 0.1875
- w_down: bfloat16 [6912, 1152], P('tensor', 'dp'), may hold values from -0.078125 to 0.078125
- gain_pre_attn: bfloat16 [1152], P(('dp', 'tensor')), may hold values from 0.5 to 1.5
- gain_post_attn: bfloat16 [1152], P(('dp', 'tensor')), may hold values from 0.5 to 1.5
- gain_pre_ffn: bfloat16 [1152], P(('dp', 'tensor')), may hold values from 0.5 to 1.5
- gain_post_ffn: bfloat16 [1152], P(('dp', 'tensor')), may hold values from 0.5 to 1.5
- gain_query: bfloat16 [256], P(('dp', 'tensor')), may hold values from 0.5 to 1.5
- gain_key: bfloat16 [256], P(('dp', 'tensor')), may hold values from 0.5 to 1.5
Outputs:
- block_out: float32 [4096, 1152], P(('dp', 'tensor'))
- grad_in: float32 [4096, 1152], P(('dp', 'tensor'))
- grad_w_query: float32 [1152, 1024], P('dp', 'tensor')
- grad_w_keyval: float32 [1152, 512], P(('dp', 'tensor'))
- grad_w_out: float32 [1024, 1152], P('tensor', 'dp')
- grad_w_gate: float32 [1152, 6912], P('dp', 'tensor')
- grad_w_up: float32 [1152, 6912], P('dp', 'tensor')
- grad_w_down: float32 [6912, 1152], P('tensor', 'dp')
- grad_pre_attn: float32 [1152], P(('dp', 'tensor'))
- grad_post_attn: float32 [1152], P(('dp', 'tensor'))
- grad_pre_ffn: float32 [1152], P(('dp', 'tensor'))
- grad_post_ffn: float32 [1152], P(('dp', 'tensor'))
- grad_gain_query: float32 [256], P(('dp', 'tensor'))
- grad_gain_key: float32 [256], P(('dp', 'tensor'))
The draws below stay inside these ranges and needn't reach their ends.
Inputs may be any that keep to these rules, and one draw needn't show every extreme that they name: `segments`: document ids never fall along the stream; every document holds 1 to 3072 tokens and one holds exactly 3072.
All inputs are finite; a program needn't handle non-finite values.
Results may differ from the reference program's by a relative error of at most 0.02.
Values may be sent and summed in bfloat16 or wider, within the bound.
No kernel may reach another device: no remote copies, remote signals or barrier semaphores. Data moves between devices by JAX's collectives and lax.ppermute only.
A program may use at most 256 MiB of HBM per device.

```python
import math
import jax
import jax.numpy as jnp
import numpy as np
from jax import lax

D = 1152
HEADS = 4
HD = 256
FF = 6912
TOK_DEV = 512
TOKENS = 4096
DOC_MOST = 3072
N_DP = 8


def draw_gain_query(key, part):
    values = jax.random.uniform(key, (HD,), jnp.float32, 0.5, 1.5)
    return values.astype(jnp.bfloat16)


def draw_gain_key(key, part):
    inner_key = jax.random.fold_in(key, 7)
    values = jax.random.uniform(inner_key, (HD,), jnp.float32, 0.5, 1.5)
    return values.astype(jnp.bfloat16)


def levels(key, dims, cuts, smallest, largest):
    factor_of, own = 1.0, jax.random.fold_in(key, 6)
    for dim, parts in cuts:
        draws = jnp.exp(jax.random.uniform(jax.random.fold_in(own, dim), (parts,), jnp.float32, smallest / len(cuts), largest / len(cuts)))
        factor_of = factor_of * jnp.repeat(draws, dims[dim] // parts).reshape([-1 if axis == dim else 1 for axis in range(len(dims))])
    return factor_of


def split_up(number_of, total, bound, slope):
    loads = [(1 << 20) // math.isqrt(standing ** slope) + 1 for standing in range(2, number_of + 1)]
    surplus, counts = total - bound - (number_of - 1), [1] * (number_of - 1)
    while surplus > 0:
        free = [i for i in range(number_of - 1) if counts[i] < bound]
        mass, left = sum([loads[i] for i in free]), surplus
        for i in free:
            addition = min(bound - counts[i], max(1, left * loads[i] // mass), surplus)
            counts[i] = counts[i] + addition
            surplus = surplus - addition
    return np.array([bound] + counts)


def ragged(key, count, total, most, slope):
    if count == 2:
        one = jax.random.randint(key, (), max(1, total - most), min(most, total - 1) + 1)
        return jnp.stack([one, total - one])
    sizes = jnp.asarray(split_up(count, total, most, slope), jnp.int32)
    pairs = (count - 1) // 2
    giver, taker = sizes[1:1 + 2 * pairs:2], sizes[2:2 + 2 * pairs:2]
    slack = jnp.minimum(giver - 1, most - taker)
    shifted = jax.random.randint(jax.random.fold_in(key, 1), (pairs,), 0, 1 << 20) % (slack + 1)
    sizes = sizes.at[1:1 + 2 * pairs:2].set(giver - shifted).at[2:2 + 2 * pairs:2].set(taker + shifted)
    return sizes[jax.random.permutation(jax.random.fold_in(key, 2), count)]


def centred(stream_key, shape, scale, most, cuts=(), kind=jnp.bfloat16):
    loudness = levels(stream_key, shape, cuts, -0.22, 0.18) if cuts else 1.0
    entries = jax.random.normal(stream_key, shape, jnp.float32) * scale * loudness
    return jnp.minimum(jnp.maximum(entries, -most), most).astype(kind)


def setup_inputs(seed: int = 0) -> dict:
    splits = jax.random.split(jax.random.key(seed), 16)
    block_in = centred(splits[0], (TOKENS, D), 1.0, 6.0, ((0, 32),), jnp.float32)
    out_grad = centred(splits[1], (TOKENS, D), 1.0, 6.0, ((0, 32),), jnp.float32)
    segments = jnp.searchsorted(jnp.cumsum(ragged(splits[2], N_DP, TOKENS, DOC_MOST, 2)), jnp.arange(TOKENS), side="right").astype(jnp.int32)
    w_query = centred(splits[3], (D, HEADS * HD), D ** -0.5, 0.1875, ((0, 8), (1, 4)))
    w_keyval = centred(splits[4], (D, 2 * HD), D ** -0.5, 0.1875, ((0, 32),))
    w_out = centred(splits[5], (HEADS * HD, D), (HEADS * HD) ** -0.5, 0.1875, ((0, 4), (1, 8)))
    w_gate = centred(splits[6], (D, FF), D ** -0.5, 0.1875, ((0, 8), (1, 4)))
    w_up = centred(splits[7], (D, FF), D ** -0.5, 0.1875, ((0, 8), (1, 4)))
    w_down = centred(splits[8], (FF, D), FF ** -0.5, 0.078125, ((0, 4), (1, 8)))
    gain_pre_attn = jnp.clip(1.0 + 0.1 * jax.random.normal(splits[9], (D,), jnp.float32), 0.5, 1.5).astype(jnp.bfloat16)
    gain_post_attn = jnp.clip(1.0 + 0.1 * jax.random.normal(splits[10], (D,), jnp.float32), 0.5, 1.5).astype(jnp.bfloat16)
    gain_pre_ffn = jnp.clip(1.0 + 0.1 * jax.random.normal(splits[11], (D,), jnp.float32), 0.5, 1.5).astype(jnp.bfloat16)
    gain_post_ffn = jnp.clip(1.0 + 0.1 * jax.random.normal(splits[12], (D,), jnp.float32), 0.5, 1.5).astype(jnp.bfloat16)
    gain_query = draw_gain_query(jax.random.fold_in(splits[15], 71), 0)
    gain_key = draw_gain_key(jax.random.fold_in(splits[15], 71), 0)
    return {"block_in": block_in, "out_grad": out_grad, "segments": segments, "w_query": w_query, "w_keyval": w_keyval, "w_out": w_out, "w_gate": w_gate, "w_up": w_up, "w_down": w_down, "gain_pre_attn": gain_pre_attn, "gain_post_attn": gain_post_attn, "gain_pre_ffn": gain_pre_ffn, "gain_post_ffn": gain_post_ffn, "gain_query": gain_query, "gain_key": gain_key}


EPSILON = 1e-06
ROPE_BASE = 1000000.0
QUERY_SCALE = 0.0625
MASKED = -1e+30
GELU_COEF = 0.7978845608028654
GELU_CUBIC = 0.044715

def rms_forward(values, scales):
    inverse = lax.rsqrt(lax.optimization_barrier(jnp.mean(values * values, axis=-1, keepdims=True)) + EPSILON)
    return (values * inverse * scales, inverse)

def rms_backward(values, inverse, scales, upstream):
    weighted = upstream * scales
    inner_mean = lax.optimization_barrier(jnp.mean(values * weighted, axis=-1, keepdims=True))
    grad_values = inverse * weighted - values * (inverse * inverse * inverse) * inner_mean
    grad_scales = lax.optimization_barrier(jnp.sum((upstream * values * inverse).reshape(-1, values.shape[-1]), axis=0))
    return (grad_values, grad_scales)

def gelu_pair(values):
    inside = GELU_COEF * (values + GELU_CUBIC * values * values * values)
    tangent = jnp.tanh(inside)
    output = 0.5 * values * (1.0 + tangent)
    derivative = 0.5 * (1.0 + tangent) + 0.5 * values * (1.0 - tangent * tangent) * GELU_COEF * (1.0 + 3.0 * GELU_CUBIC * values * values)
    return (output, derivative)

def rotate_half(values):
    halfway = values.shape[-1] // 2
    return jnp.concatenate([-values[..., halfway:], values[..., :halfway]], axis=-1)

def rope_tables(positions):
    halfway = HD // 2
    frequency = ROPE_BASE ** (-2.0 * jnp.arange(halfway, dtype=jnp.float32) / HD)
    angles = positions.astype(jnp.float32)[:, None] * frequency[None, :]
    angles = jnp.concatenate([angles, angles], axis=1)
    return (jnp.cos(angles), jnp.sin(angles))

def apply_rope(values, cosine, sine_part):
    return values * cosine + rotate_half(values) * sine_part

def rope_back(upstream, cosine, sine_part):
    return upstream * cosine - rotate_half(upstream * sine_part)

def widen(values):
    return lax.optimization_barrier(values).astype(jnp.float32)

def rounded(values):
    return widen(values.astype(jnp.bfloat16))

def reference(block_in, out_grad, segments, w_query, w_keyval, w_out, w_gate, w_up, w_down, gain_pre_attn, gain_post_attn, gain_pre_ffn, gain_post_ffn, gain_query, gain_key):
    block_count = TOKENS // TOK_DEV
    scale_pre_attn = gain_pre_attn.astype(jnp.float32)
    scale_post_attn = gain_post_attn.astype(jnp.float32)
    scale_pre_ffn = gain_pre_ffn.astype(jnp.float32)
    scale_post_ffn = gain_post_ffn.astype(jnp.float32)
    scale_query = gain_query.astype(jnp.float32)
    scale_key = gain_key.astype(jnp.float32)
    normed_in, inv_in = rms_forward(block_in, scale_pre_attn)
    normed_bf = normed_in.astype(jnp.bfloat16)
    queries = jnp.dot(normed_bf, w_query, preferred_element_type=jnp.float32).reshape(TOKENS, HEADS, HD)
    keyval = jnp.dot(normed_bf, w_keyval, preferred_element_type=jnp.float32)
    cosine, sine_part = rope_tables(jnp.arange(TOKENS, dtype=jnp.int32))
    query_norm, inv_query = rms_forward(queries, scale_query)
    query_rot = (apply_rope(query_norm, cosine[:, None, :], sine_part[:, None, :]) * QUERY_SCALE).astype(jnp.bfloat16)
    key_proj = keyval[:, :HD]
    key_norm, inv_key = rms_forward(key_proj, scale_key)
    key_rot = apply_rope(key_norm, cosine, sine_part).astype(jnp.bfloat16)
    value_proj = keyval[:, HD:].astype(jnp.bfloat16)
    key_wide = widen(key_rot)
    value_wide = widen(value_proj)
    key_index = jnp.arange(TOKENS, dtype=jnp.int32)

    def block_mask(block_id):
        row_index = block_id * TOK_DEV + jnp.arange(TOK_DEV, dtype=jnp.int32)
        row_segment = lax.dynamic_slice_in_dim(segments, block_id * TOK_DEV, TOK_DEV)
        return (row_segment[:, None] == segments[None, :]) & (key_index[None, :] <= row_index[:, None])

    def attend(block_id):
        query_block = widen(lax.dynamic_slice_in_dim(query_rot, block_id * TOK_DEV, TOK_DEV, 0))
        visible = block_mask(block_id)[None]
        scores = jnp.where(visible, jnp.einsum('qhd,kd->hqk', query_block, key_wide), MASKED)
        row_max = lax.optimization_barrier(jnp.max(scores, axis=-1, keepdims=True))
        weights = jnp.where(visible, jnp.exp(scores - row_max), 0.0)
        row_sum = lax.optimization_barrier(jnp.sum(weights, axis=-1))
        mixed = jnp.einsum('hqk,kd->qhd', rounded(weights), value_wide)
        return (mixed / jnp.transpose(row_sum)[:, :, None], row_max[..., 0] + jnp.log(row_sum))
    mixed_all, log_all = lax.map(attend, jnp.arange(block_count, dtype=jnp.int32))
    mixed_tok = mixed_all.reshape(TOKENS, HEADS * HD).astype(jnp.bfloat16)
    log_norm = jnp.transpose(log_all, (0, 2, 1)).reshape(TOKENS, HEADS)
    attn_out = jnp.dot(mixed_tok, w_out, preferred_element_type=jnp.float32)
    attn_norm, inv_attn = rms_forward(attn_out, scale_post_attn)
    resid_mid = block_in + attn_norm

    def ffn_step(totals, pair):
        resid_block, grad_block = pair
        normed_mid, inv_mid = rms_forward(resid_block, scale_pre_ffn)
        mid_bf = normed_mid.astype(jnp.bfloat16)
        gate_pre = jnp.dot(mid_bf, w_gate, preferred_element_type=jnp.float32)
        up_proj = jnp.dot(mid_bf, w_up, preferred_element_type=jnp.float32)
        gate_act, gate_deriv = gelu_pair(gate_pre)
        hidden = (gate_act * up_proj).astype(jnp.bfloat16)
        ffn_out = jnp.dot(hidden, w_down, preferred_element_type=jnp.float32)
        ffn_norm, inv_ffn = rms_forward(ffn_out, scale_post_ffn)
        grad_ffn, grad_post = rms_backward(ffn_out, inv_ffn, scale_post_ffn, grad_block)
        grad_ffn_bf = grad_ffn.astype(jnp.bfloat16)
        grad_hidden = jnp.dot(grad_ffn_bf, w_down.T, preferred_element_type=jnp.float32)
        grad_gate = (grad_hidden * up_proj * gate_deriv).astype(jnp.bfloat16)
        grad_up = (grad_hidden * gate_act).astype(jnp.bfloat16)
        grad_mid = jnp.dot(grad_gate, w_gate.T, preferred_element_type=jnp.float32) + jnp.dot(grad_up, w_up.T, preferred_element_type=jnp.float32)
        grad_resid, grad_pre = rms_backward(resid_block, inv_mid, scale_pre_ffn, grad_mid)
        totals = (totals[0] + jnp.dot(mid_bf.T, grad_gate, preferred_element_type=jnp.float32), totals[1] + jnp.dot(mid_bf.T, grad_up, preferred_element_type=jnp.float32), totals[2] + jnp.dot(hidden.T, grad_ffn_bf, preferred_element_type=jnp.float32), totals[3] + grad_pre, totals[4] + grad_post)
        return (totals, (resid_block + ffn_norm, grad_block + grad_resid))
    start_totals = (jnp.zeros((D, FF), jnp.float32), jnp.zeros((D, FF), jnp.float32), jnp.zeros((FF, D), jnp.float32), jnp.zeros((D,), jnp.float32), jnp.zeros((D,), jnp.float32))
    totals, (out_blocks, grad_blocks) = lax.scan(ffn_step, start_totals, (resid_mid.reshape(block_count, TOK_DEV, D), out_grad.reshape(block_count, TOK_DEV, D)))
    block_out = out_blocks.reshape(TOKENS, D)
    grad_resid_mid = grad_blocks.reshape(TOKENS, D)
    grad_attn, grad_post_attn = rms_backward(attn_out, inv_attn, scale_post_attn, grad_resid_mid)
    grad_attn_bf = grad_attn.astype(jnp.bfloat16)
    grad_w_out = jnp.dot(mixed_tok.T, grad_attn_bf, preferred_element_type=jnp.float32)
    grad_mixed = jnp.dot(grad_attn_bf, w_out.T, preferred_element_type=jnp.float32).astype(jnp.bfloat16)
    grad_mixed_wide = widen(grad_mixed).reshape(TOKENS, HEADS, HD)
    mixed_wide = widen(mixed_tok).reshape(TOKENS, HEADS, HD)
    delta_all = lax.optimization_barrier(jnp.sum(grad_mixed_wide * mixed_wide, axis=-1))

    def back_step(carry, block_id):
        grad_keys, grad_values = carry
        begin = block_id * TOK_DEV
        query_block = widen(lax.dynamic_slice_in_dim(query_rot, begin, TOK_DEV, 0))
        grad_block = lax.dynamic_slice_in_dim(grad_mixed_wide, begin, TOK_DEV, 0)
        log_block = jnp.transpose(lax.dynamic_slice_in_dim(log_norm, begin, TOK_DEV, 0))
        delta_block = jnp.transpose(lax.dynamic_slice_in_dim(delta_all, begin, TOK_DEV, 0))
        visible = block_mask(block_id)[None]
        scores = jnp.einsum('qhd,kd->hqk', query_block, key_wide)
        weights = jnp.where(visible, jnp.exp(scores - log_block[:, :, None]), 0.0)
        grad_prob = jnp.einsum('qhd,kd->hqk', grad_block, value_wide)
        grad_score = rounded(weights * (grad_prob - delta_block[:, :, None]))
        grad_query = jnp.einsum('hqk,kd->qhd', grad_score, key_wide)
        grad_keys = grad_keys + jnp.einsum('hqk,qhd->kd', grad_score, query_block)
        grad_values = grad_values + jnp.einsum('hqk,qhd->kd', rounded(weights), grad_block)
        return ((grad_keys, grad_values), grad_query)
    start_kv = (jnp.zeros((TOKENS, HD), jnp.float32), jnp.zeros((TOKENS, HD), jnp.float32))
    (grad_keys, grad_values), grad_query_all = lax.scan(back_step, start_kv, jnp.arange(block_count, dtype=jnp.int32))
    grad_query_rot = grad_query_all.reshape(TOKENS, HEADS, HD)
    grad_query_norm = rope_back(grad_query_rot, cosine[:, None, :], sine_part[:, None, :]) * QUERY_SCALE
    grad_queries, grad_gain_query = rms_backward(queries, inv_query, scale_query, grad_query_norm)
    grad_key_norm = rope_back(grad_keys, cosine, sine_part)
    grad_key_proj, grad_gain_key = rms_backward(key_proj, inv_key, scale_key, grad_key_norm)
    grad_query_bf = grad_queries.reshape(TOKENS, HEADS * HD).astype(jnp.bfloat16)
    grad_keyval_bf = jnp.concatenate([grad_key_proj, grad_values], axis=1).astype(jnp.bfloat16)
    grad_w_query = jnp.dot(normed_bf.T, grad_query_bf, preferred_element_type=jnp.float32)
    grad_w_keyval = jnp.dot(normed_bf.T, grad_keyval_bf, preferred_element_type=jnp.float32)
    grad_normed = jnp.dot(grad_query_bf, w_query.T, preferred_element_type=jnp.float32) + jnp.dot(grad_keyval_bf, w_keyval.T, preferred_element_type=jnp.float32)
    grad_in_norm, grad_pre_attn = rms_backward(block_in, inv_in, scale_pre_attn, grad_normed)
    grad_in = grad_resid_mid + grad_in_norm
    return (block_out, grad_in, grad_w_query, grad_w_keyval, grad_w_out, totals[0], totals[1], totals[2], grad_pre_attn, grad_post_attn, totals[3], totals[4], grad_gain_query, grad_gain_key)
```

```python
import jax
import jax.numpy as jnp
from jax import lax
from jax.sharding import PartitionSpec as P

HD = 256

EPSILON = 1e-06
ROPE_BASE = 1000000.0
QUERY_SCALE = 0.0625
MASKED = -1e30
GELU_COEF = 0.7978845608028654
GELU_CUBIC = 0.044715
BF = jnp.bfloat16
F32 = jnp.float32


def rms_inverse(values):
    return lax.rsqrt(jnp.mean(values * values, axis=-1, keepdims=True) + EPSILON)


def rms_backward(values, inverse, scales, upstream):
    weighted = upstream * scales
    inner_mean = jnp.mean(values * weighted, axis=-1, keepdims=True)
    grad_values = inverse * weighted - values * (inverse * inverse * inverse) * inner_mean
    grad_scales = jnp.sum(upstream * values * inverse, axis=0)
    return (grad_values, grad_scales)


def gelu_pair(values):
    inside = GELU_COEF * (values + GELU_CUBIC * values * values * values)
    tangent = jnp.tanh(inside)
    output = 0.5 * values * (1.0 + tangent)
    derivative = 0.5 * (1.0 + tangent) + 0.5 * values * (1.0 - tangent * tangent) * GELU_COEF * (
        1.0 + 3.0 * GELU_CUBIC * values * values
    )
    return (output, derivative)


def rotate_half(values):
    halfway = values.shape[-1] // 2
    return jnp.concatenate([-values[..., halfway:], values[..., :halfway]], axis=-1)


def rope_tables(positions):
    halfway = HD // 2
    frequency = ROPE_BASE ** (-2.0 * jnp.arange(halfway, dtype=F32) / HD)
    angles = positions.astype(F32)[:, None] * frequency[None, :]
    angles = jnp.concatenate([angles, angles], axis=1)
    return (jnp.cos(angles), jnp.sin(angles))


def apply_rope(values, cosine, sine_part):
    return values * cosine + rotate_half(values) * sine_part


def rope_back(upstream, cosine, sine_part):
    return upstream * cosine - rotate_half(upstream * sine_part)


def dot(left, right):
    return jnp.dot(left, right, preferred_element_type=F32)


def contract_first(left, right):
    return lax.dot_general(left, right, (((0,), (0,)), ((), ())), preferred_element_type=F32)


def contract_last(left, right):
    return lax.dot_general(left, right, (((1,), (1,)), ((), ())), preferred_element_type=F32)


def ring(value, steps):
    count = lax.axis_size("tensor")
    return lax.ppermute(value, "tensor", [(s, (s + steps) % count) for s in range(count)])


def swap(value, mask):
    count = lax.axis_size("dp")
    return lax.ppermute(value, "dp", [(s, s ^ mask) for s in range(count)])


def gather_rows(values):
    count = lax.axis_size("tensor")
    return jnp.concatenate([values] + [ring(values, k) for k in range(1, count)], axis=0)


def scatter_rows(partial):
    count = lax.axis_size("tensor")
    length = partial.shape[0] // count
    total = partial[:length]
    for k in range(1, count):
        piece = partial[k * length : (k + 1) * length].astype(BF)
        total = total + ring(piece, -k).astype(F32)
    return total


def gather_blocks(values):
    count = lax.axis_size("dp")
    near = [values] + [swap(values, 2 * k) for k in range(1, count // 2)]
    far = [swap(piece, 1) for piece in near]
    return jnp.stack(near + far)


def block_order():
    count = lax.axis_size("dp")
    return [2 * k for k in range(count // 2)] + [2 * k + 1 for k in range(count // 2)]


def scatter_blocks(blocks):
    count = lax.axis_size("dp")
    own = lax.axis_index("dp")

    def pick(mask):
        return lax.dynamic_index_in_dim(blocks, own ^ mask, 0, keepdims=False)

    far = swap(jnp.stack([pick(2 * k + 1) for k in range(count // 2)]), 1).astype(F32)
    paired = [far[k] + pick(2 * k).astype(F32) for k in range(count // 2)]
    total = paired[0]
    for k in range(1, count // 2):
        total = total + swap(paired[k].astype(BF), 2 * k).astype(F32)
    return total


def three_terms(values):
    first = lax.reduce_precision(values, 8, 7)
    rest = values - first
    second = lax.reduce_precision(rest, 8, 7)
    third = lax.reduce_precision(rest - second, 8, 7)
    return jnp.concatenate([first, second, third]).astype(BF)


def with_vector(rows, vector):
    terms = three_terms(vector).reshape(-1, HD)
    padding = jnp.zeros((-terms.shape[0] % 16, HD), BF)
    return jnp.concatenate([rows, terms, padding], axis=0)


def split_vector(stacked, length):
    count = stacked.shape[0]
    extra = length // HD
    rows = stacked[:, :length].reshape(count * length, HD)
    terms = stacked[:, length : length + 3 * extra].astype(F32).reshape(count, 3, length)
    return rows, jnp.sum(terms, axis=1).reshape(count * length)


def per_device(
    block_in,
    out_grad,
    segments,
    w_query,
    w_keyval,
    w_out,
    w_gate,
    w_up,
    w_down,
    gain_pre_attn,
    gain_post_attn,
    gain_pre_ffn,
    gain_post_ffn,
    gain_query,
    gain_key,
):
    splits = lax.axis_size("tensor")
    blocks = lax.axis_size("dp")
    row_count, width = block_in.shape
    block_len = row_count * splits
    own_block = lax.axis_index("dp")
    own_part = lax.axis_index("tensor")
    small_rows = w_keyval.shape[0]
    weight_rows = w_query.shape[0]
    big = gain_pre_attn.shape[0]
    little = gain_query.shape[0]
    per_owner = 4 * big + 2 * little

    inv_in = rms_inverse(block_in)
    unit_in = block_in * inv_in
    unit_all = gather_rows(unit_in.astype(BF))
    gains_own = jnp.concatenate(
        [gain_pre_attn, gain_post_attn, gain_pre_ffn, gain_post_ffn, gain_query, gain_key]
    )
    gains_row = jnp.pad(gains_own, (0, 2 * HD - per_owner))[None, :]
    small = jnp.concatenate([w_keyval, gains_row], axis=0)
    small = lax.all_gather(small, "tensor", axis=0, tiled=False)
    keyval_rows = small[:, :small_rows].reshape(weight_rows, 2 * HD)
    gains_rows = jnp.pad(
        small[:, small_rows, :per_owner].reshape(-1), (0, 4 * HD - splits * per_owner)
    )[None, :]
    packed = jnp.concatenate([w_query, w_out.T, keyval_rows], axis=1)
    packed = jnp.concatenate([packed, gains_rows, jnp.zeros((7, 4 * HD), BF)], axis=0)
    w_gate, w_up, w_down, packed = lax.optimization_barrier((w_gate, w_up, w_down, packed))
    packed = lax.all_gather(packed, "dp", axis=0, tiled=False)
    weights_in = packed[:, :weight_rows]
    query_full = weights_in[:, :, :HD].reshape(width, HD)
    out_full = weights_in[:, :, HD : 2 * HD].reshape(width, HD)
    keyval_full = weights_in[:, :, 2 * HD :].reshape(width, 2 * HD)
    gains = packed[:, weight_rows, : splits * per_owner].astype(F32)
    gains = gains.reshape(blocks * splits, per_owner)
    scale_pre_attn = gains[:, :big].reshape(width)
    scale_post_attn = gains[:, big : 2 * big].reshape(width)
    scale_pre_ffn = gains[:, 2 * big : 3 * big].reshape(width)
    scale_post_ffn = gains[:, 3 * big : 4 * big].reshape(width)
    scale_query = gains[:, 4 * big : 4 * big + little].reshape(HD)
    scale_key = gains[:, 4 * big + little :].reshape(HD)
    gate_full = lax.all_gather(w_gate, "dp", axis=0, tiled=True)
    up_full = lax.all_gather(w_up, "dp", axis=0, tiled=True)
    down_full = lax.all_gather(w_down, "dp", axis=1, tiled=True)

    part_order = [(own_part - k) % splits for k in range(splits)]
    offsets = jnp.concatenate(
        [part * row_count + jnp.arange(row_count, dtype=jnp.int32) for part in part_order]
    )
    seg_parts = segments.reshape(blocks, splits, row_count)
    seg_parts = jnp.concatenate(
        [lax.dynamic_index_in_dim(seg_parts, part, 1, keepdims=False) for part in part_order], axis=1
    )
    own_segment = lax.dynamic_index_in_dim(seg_parts, own_block, 0, keepdims=False)
    own_index = own_block * block_len + offsets
    order = block_order()
    all_segment = jnp.concatenate(
        [lax.dynamic_index_in_dim(seg_parts, own_block ^ m, 0, keepdims=False) for m in order]
    )
    all_index = jnp.concatenate([(own_block ^ m) * block_len + offsets for m in order])

    gathered_in = (unit_all.astype(F32) * scale_pre_attn).astype(BF)
    queries = dot(gathered_in, query_full)
    keyval = dot(gathered_in, keyval_full)
    cosine, sine_part = rope_tables(own_index)
    key_proj = keyval[:, :HD]
    inv_key = rms_inverse(key_proj)
    key_rot = apply_rope(key_proj * inv_key * scale_key, cosine, sine_part).astype(BF)
    value_proj = keyval[:, HD:].astype(BF)
    keyval_all = gather_blocks(jnp.concatenate([key_rot, value_proj], axis=1))
    key_all = keyval_all[:, :, :HD].reshape(blocks * block_len, HD)
    value_all = keyval_all[:, :, HD:].reshape(blocks * block_len, HD)
    inv_query = rms_inverse(queries)
    query_rot = (
        apply_rope(queries * inv_query * scale_query, cosine, sine_part) * QUERY_SCALE
    ).astype(BF)

    visible = (own_segment[:, None] == all_segment[None, :]) & (
        all_index[None, :] <= own_index[:, None]
    )
    scores = jnp.where(visible, contract_last(query_rot, key_all), MASKED)
    row_max = jnp.max(scores, axis=1)
    weights = jnp.where(visible, jnp.exp(scores - row_max[:, None]), 0.0)
    row_sum = jnp.sum(weights, axis=1)
    row_acc = dot(weights.astype(BF), value_all)
    log_norm = row_max + jnp.log(row_sum)
    mixed = (row_acc / row_sum[:, None]).astype(BF)
    query_part = gather_blocks(with_vector(query_rot, log_norm))
    attn_out = scatter_rows(contract_last(mixed, out_full))
    inv_attn = rms_inverse(attn_out)
    resid_mid = block_in + attn_out * inv_attn * scale_post_attn

    inv_mid = rms_inverse(resid_mid)
    gathered_mid = gather_rows((resid_mid * inv_mid * scale_pre_ffn).astype(BF))
    gate_pre = dot(gathered_mid, gate_full)
    up_proj = dot(gathered_mid, up_full)
    gate_act, gate_deriv = gelu_pair(gate_pre)
    hidden = (gate_act * up_proj).astype(BF)
    ffn_out = scatter_rows(dot(hidden, down_full))
    inv_ffn = rms_inverse(ffn_out)
    block_out = resid_mid + ffn_out * inv_ffn * scale_post_ffn
    grad_ffn, grad_post_ffn = rms_backward(ffn_out, inv_ffn, scale_post_ffn, out_grad)
    grad_ffn_all = gather_rows(grad_ffn.astype(BF))
    grad_hidden = contract_last(grad_ffn_all, down_full)
    grad_gate = (grad_hidden * up_proj * gate_deriv).astype(BF)
    grad_up = (grad_hidden * gate_act).astype(BF)
    grad_mid = scatter_rows(contract_last(grad_gate, gate_full) + contract_last(grad_up, up_full))
    grad_w_down = contract_first(hidden, grad_ffn_all).astype(BF)
    owned_down = lax.psum_scatter(grad_w_down, "dp", scatter_dimension=1, tiled=True)
    grad_w_gate = contract_first(gathered_mid, grad_gate).astype(BF)
    owned_gate = lax.psum_scatter(grad_w_gate, "dp", scatter_dimension=0, tiled=True)
    grad_w_up = contract_first(gathered_mid, grad_up).astype(BF)
    owned_up = lax.psum_scatter(grad_w_up, "dp", scatter_dimension=0, tiled=True)
    grad_resid, grad_pre_ffn = rms_backward(resid_mid, inv_mid, scale_pre_ffn, grad_mid)
    grad_resid_mid = out_grad + grad_resid

    grad_attn, grad_post_attn = rms_backward(attn_out, inv_attn, scale_post_attn, grad_resid_mid)
    grad_attn_all = gather_rows(grad_attn.astype(BF))
    grad_mixed = dot(grad_attn_all, out_full).astype(BF)
    delta = jnp.sum(grad_mixed.astype(F32) * mixed.astype(F32), axis=1)
    grad_part = gather_blocks(with_vector(grad_mixed, delta))
    grad_w_out = contract_first(grad_attn_all, mixed).astype(BF)
    owned_out = lax.psum_scatter(grad_w_out, "dp", scatter_dimension=0, tiled=True)

    scores = contract_last(query_rot, key_all)
    weights = jnp.where(visible, jnp.exp(scores - log_norm[:, None]), 0.0)
    grad_prob = contract_last(grad_mixed, value_all)
    grad_score = (weights * (grad_prob - delta[:, None])).astype(BF)
    grad_query_rot = dot(grad_score, key_all)

    part_query, part_log = split_vector(query_part, block_len)
    part_grad, part_delta = split_vector(grad_part, block_len)
    shown = (own_segment[:, None] == all_segment[None, :]) & (
        own_index[:, None] <= all_index[None, :]
    )
    scores = contract_last(key_rot, part_query)
    weights = jnp.where(shown, jnp.exp(scores - part_log[None, :]), 0.0)
    grad_prob = contract_last(value_proj, part_grad)
    grad_score = (weights * (grad_prob - part_delta[None, :])).astype(BF)
    grad_keyval_part = jnp.concatenate(
        [dot(grad_score, part_query), dot(weights.astype(BF), part_grad)], axis=1
    )
    grad_keyval_rows = scatter_rows(grad_keyval_part)

    grad_query_norm = rope_back(grad_query_rot, cosine, sine_part) * QUERY_SCALE
    grad_queries, grad_gain_query = rms_backward(queries, inv_query, scale_query, grad_query_norm)
    grad_query_bf = grad_queries.astype(BF)
    grad_w_query = contract_first(gathered_in, grad_query_bf)
    grad_key_norm = rope_back(grad_keyval_rows[:, :HD], cosine[:row_count], sine_part[:row_count])
    grad_key_proj, grad_gain_key = rms_backward(
        key_proj[:row_count], inv_key[:row_count], scale_key, grad_key_norm
    )
    grad_keyval_bf = jnp.concatenate([grad_key_proj, grad_keyval_rows[:, HD:]], axis=1).astype(BF)
    grad_w_keyval = contract_first(gathered_in, gather_rows(grad_keyval_bf))
    normed_query = contract_last(grad_query_bf, query_full)
    normed_keyval = contract_last(grad_keyval_bf, keyval_full)
    grad_pre_attn = jnp.sum(normed_query * unit_all.astype(F32), axis=0) + jnp.sum(
        normed_keyval * unit_in, axis=0
    )
    grad_normed = scatter_rows(normed_query) + normed_keyval
    grad_in_norm, _ = rms_backward(block_in, inv_in, scale_pre_attn, grad_normed)
    grad_in = grad_resid_mid + grad_in_norm

    gain_grads = jnp.concatenate(
        [
            g.reshape(blocks, splits, -1)
            for g in (
                grad_pre_attn,
                grad_post_attn,
                grad_pre_ffn,
                grad_post_ffn,
                grad_gain_query,
                grad_gain_key,
            )
        ],
        axis=2,
    )

    def gains_of(part):
        return lax.dynamic_index_in_dim(gain_grads, part, 1, keepdims=False)

    gains_sum = gains_of(own_part)
    for k in range(1, splits):
        gains_sum = gains_sum + ring(gains_of((own_part - k) % splits), -k)
    gains_high = lax.reduce_precision(gains_sum, 8, 7)
    gains_pair = jnp.stack([gains_high, gains_sum - gains_high], axis=1).astype(BF)
    gains_pair = jnp.pad(gains_pair, ((0, 0), (0, 6), (0, HD - per_owner)))
    keyval_own = lax.dynamic_index_in_dim(
        grad_w_keyval.astype(BF).reshape(blocks, splits, small_rows, 2 * HD),
        own_part,
        1,
        keepdims=False,
    )
    owned = scatter_blocks(
        jnp.concatenate(
            [
                grad_w_query.astype(BF).reshape(blocks, weight_rows, HD),
                keyval_own[:, :, :HD],
                keyval_own[:, :, HD:],
                gains_pair,
            ],
            axis=1,
        )
    )
    owned_query = owned[:weight_rows]
    after = weight_rows + small_rows
    owned_keyval = jnp.concatenate(
        [owned[weight_rows:after], owned[after : after + small_rows]], axis=1
    )
    after = after + small_rows
    owned_gains = owned[after, :per_owner] + owned[after + 1, :per_owner]
    return (
        block_out,
        grad_in,
        owned_query,
        owned_keyval,
        owned_out.astype(F32).T,
        owned_gate.astype(F32),
        owned_up.astype(F32),
        owned_down.astype(F32),
        owned_gains[:big],
        owned_gains[big : 2 * big],
        owned_gains[2 * big : 3 * big],
        owned_gains[3 * big : 4 * big],
        owned_gains[4 * big : 4 * big + little],
        owned_gains[4 * big + little :],
    )


def solution(mesh):
    return jax.shard_map(
        per_device,
        mesh=mesh,
        in_specs=(
            P(("dp", "tensor"), None),
            P(("dp", "tensor"), None),
            P(),
            P("dp", "tensor"),
            P(("dp", "tensor"), None),
            P("tensor", "dp"),
            P("dp", "tensor"),
            P("dp", "tensor"),
            P("tensor", "dp"),
            P(("dp", "tensor")),
            P(("dp", "tensor")),
            P(("dp", "tensor")),
            P(("dp", "tensor")),
            P(("dp", "tensor")),
            P(("dp", "tensor")),
        ),
        out_specs=(
            P(("dp", "tensor"), None),
            P(("dp", "tensor"), None),
            P("dp", "tensor"),
            P(("dp", "tensor"), None),
            P("tensor", "dp"),
            P("dp", "tensor"),
            P("dp", "tensor"),
            P("tensor", "dp"),
            P(("dp", "tensor")),
            P(("dp", "tensor")),
            P(("dp", "tensor")),
            P(("dp", "tensor")),
            P(("dp", "tensor")),
            P(("dp", "tensor")),
        ),
        check_vma=False,
    )
```

```python
import jax
import jax.numpy as jnp
from jax import lax
from jax.experimental import pallas as pl
from jax.experimental.layout import Layout, with_layout_constraint
from jax.experimental.pallas import tpu as pltpu
from jax.sharding import PartitionSpec as P

HD = 256

EPSILON = 1e-06
ROPE_BASE = 1000000.0
QUERY_SCALE = 0.0625
MASKED = -1e30
GELU_COEF = 0.7978845608028654
GELU_CUBIC = 0.044715
BF = jnp.bfloat16
F32 = jnp.float32


def rms_inverse(values):
    return lax.rsqrt(jnp.mean(values * values, axis=-1, keepdims=True) + EPSILON)


def rms_backward(values, inverse, scales, upstream):
    weighted = upstream * scales
    inner_mean = jnp.mean(values * weighted, axis=-1, keepdims=True)
    grad_values = inverse * weighted - values * (inverse * inverse * inverse) * inner_mean
    grad_scales = jnp.sum(upstream * values * inverse, axis=0)
    return (grad_values, grad_scales)


def gelu_pair(values):
    inside = GELU_COEF * (values + GELU_CUBIC * values * values * values)
    tangent = jnp.tanh(inside)
    output = 0.5 * values * (1.0 + tangent)
    derivative = 0.5 * (1.0 + tangent) + 0.5 * values * (1.0 - tangent * tangent) * GELU_COEF * (
        1.0 + 3.0 * GELU_CUBIC * values * values
    )
    return (output, derivative)


def rotate_half(values):
    halfway = values.shape[-1] // 2
    return jnp.concatenate([-values[..., halfway:], values[..., :halfway]], axis=-1)


def rope_tables(positions):
    halfway = HD // 2
    frequency = ROPE_BASE ** (-2.0 * jnp.arange(halfway, dtype=F32) / HD)
    angles = positions.astype(F32)[:, None] * frequency[None, :]
    angles = jnp.concatenate([angles, angles], axis=1)
    return (jnp.cos(angles), jnp.sin(angles))


def apply_rope(values, cosine, sine_part):
    return values * cosine + rotate_half(values) * sine_part


def rope_back(upstream, cosine, sine_part):
    return upstream * cosine - rotate_half(upstream * sine_part)


def dot(left, right):
    return jnp.dot(left, right, preferred_element_type=F32)


def contract_first(left, right):
    return lax.dot_general(left, right, (((0,), (0,)), ((), ())), preferred_element_type=F32)


def contract_last(left, right):
    return lax.dot_general(left, right, (((1,), (1,)), ((), ())), preferred_element_type=F32)

AXES = ("dp", "tensor")
PAIR = 2


def place(device):
    return device >> 3, (device >> 2) & 1, (device >> 1) & 1, device & 1


def device_at(block, core, half, low):
    return (block << 3) | (core << 2) | (half << 1) | low


def device_count():
    return lax.axis_size("dp") * lax.axis_size("tensor")


def own_device():
    return lax.axis_index("dp") * lax.axis_size("tensor") + lax.axis_index("tensor")


def flip(value, mask):
    return lax.ppermute(value, AXES, [(s, s ^ mask) for s in range(device_count())])


def send(value, target):
    pairs = [(s, target(*place(s))) for s in range(device_count())]
    return lax.ppermute(value, AXES, [(s, t) for s, t in pairs if t is not None])


LOW, HALF, CORE, BLOCK = 1, 2, 4, 8
GROUP = (0, LOW, CORE, CORE | LOW)


def block_masks():
    return [BLOCK * k for k in range(lax.axis_size("dp") // PAIR)]


def natural(items, index):
    count, rows, columns = items.shape

    def body(index_ref, item_ref, out_ref):
        out_ref[...] = item_ref[...]

    return pl.pallas_call(
        body,
        out_shape=jax.ShapeDtypeStruct(items.shape, items.dtype),
        grid_spec=pltpu.PrefetchScalarGridSpec(
            num_scalar_prefetch=1,
            grid=(count,),
            in_specs=[pl.BlockSpec((1, rows, columns), lambda i, ref: (i ^ ref[0], 0, 0))],
            out_specs=pl.BlockSpec((1, rows, columns), lambda i, ref: (i, 0, 0)),
        ),
    )(index[None], items)


def shared_rows(near, far, device, rows):
    blocks, _, _, columns = near.shape
    count = 8 * blocks

    def body(index_ref, near_ref, far_ref, rows_ref, gains_ref, wide_ref):
        for owner in range(count):
            at = owner ^ index_ref[0]
            block, low = at >> 3, at & 3
            mine = near_ref[block, low].astype(F32)
            other = far_ref[block, low].astype(F32)
            piece = jnp.where((at & CORE) == 0, mine, other)
            wide_ref[owner * rows : (owner + 1) * rows, :] = piece[:rows]
            gains_ref[owner : owner + 1, :] = piece[rows : rows + 1]
        rows_ref[...] = wide_ref[...].astype(BF)

    return pl.pallas_call(
        body,
        out_shape=(
            jax.ShapeDtypeStruct((count * rows, columns), BF),
            jax.ShapeDtypeStruct((count, columns), F32),
        ),
        in_specs=[
            pl.BlockSpec(memory_space=pltpu.SMEM),
            pl.BlockSpec(memory_space=pltpu.VMEM),
            pl.BlockSpec(memory_space=pltpu.VMEM),
        ],
        out_specs=(
            pl.BlockSpec(memory_space=pltpu.VMEM),
            pl.BlockSpec(memory_space=pltpu.VMEM),
        ),
        scratch_shapes=[pltpu.VMEM((count * rows, columns), F32)],
    )(device[None], near, far)


def row_major(values):
    return with_layout_constraint(values, Layout(major_to_minor=(0, 1)))


def column_major(values):
    return with_layout_constraint(values, Layout(major_to_minor=(1, 0)))


def group_gather(values):
    near = flip(values, LOW)
    across = flip(values, CORE)
    return jnp.concatenate([values, near, across, flip(near, CORE)], axis=0)


def group_scatter(product, *rows):
    middle = rows[0].shape[0] // 2
    length = middle // 2
    far = flip(product(*[r[middle:] for r in rows]).astype(BF), CORE)
    near = product(*[r[:middle] for r in rows]) + far.astype(F32)
    return near[:length] + flip(near[length:].astype(BF), LOW).astype(F32)


def after(value, *others):
    return lax.optimization_barrier((value, *others))[0]


def column_gather(values):
    return jnp.concatenate([values] + [flip(values, mask) for mask in (1, 2, 3)], axis=0)


def column_scatter(product, *rows):
    middle = rows[0].shape[0] // 2
    length = middle // 2
    far = product(*[r[middle:] for r in rows]).astype(BF)
    far = [flip(far[length:], 3), flip(far[:length], 2)]
    near = product(*[r[:middle] for r in rows])
    near = near[:length] + flip(near[length:].astype(BF), 1).astype(F32)
    return near + far[0].astype(F32) + far[1].astype(F32)


def exchange_first(value):
    def target(block, core, half, low):
        if half == core:
            return device_at(block, core, 1 - half, low)
        return device_at(block, 1 - core, half, low)

    return send(value, target)


def exchange_second(value):
    def target(block, core, half, low):
        return None if half == core else device_at(block, 1 - core, 1 - half, low)

    return send(value, target)


def weight_pair(value, axis):
    _, core, half, _ = place(own_device())
    first, second = exchange_first(value), exchange_second(value)
    kept = jnp.where(half == core, value, second)
    return jnp.concatenate(
        [jnp.where(half == 0, kept, first), jnp.where(half == 0, first, kept)], axis=axis
    )


def grad_owner(pair):
    return jnp.sum(jnp.stack(grad_owner_parts(pair)), axis=0)


def grad_owner_parts(pair):
    _, core, half, _ = place(own_device())
    pair = pair.astype(BF)
    first = jnp.where(half == 0, pair[1], pair[0])
    second = jnp.where(half == 0, pair[0], pair[1])
    got = exchange_second(second)
    return [
        exchange_first_back(first).astype(F32),
        jnp.where(half == core, second, got).astype(F32),
    ]


def exchange_first_back(value):
    def target(block, core, half, low):
        if half == core:
            return device_at(block, 1 - core, half, low)
        return device_at(block, core, 1 - half, low)

    return send(value, target)


def scatter_blocks(values):
    own = own_device() >> 3
    total = lax.dynamic_index_in_dim(values, own, 0, keepdims=False).astype(F32)
    for mask in block_masks()[1:]:
        piece = lax.dynamic_index_in_dim(values, own ^ (mask // BLOCK), 0, keepdims=False)
        total = total + flip(piece.astype(BF), mask).astype(F32)
    return total


def head_gather(values):
    near = [flip(values, mask) for mask in block_masks()[1:]]
    other = flip(values, HALF)
    far = [flip(other, mask) for mask in block_masks()[1:]]
    return [values, *near, other, *far]


def token_gather(values):
    column = jnp.concatenate([values] + [flip(values, mask) for mask in (1, 2, 3)], axis=0)
    near = [column] + [flip(column, mask) for mask in block_masks()[1:]]
    return near, lambda later: near + [flip(after(piece, later), CORE) for piece in near]


def three_terms(values):
    first = lax.reduce_precision(values, 8, 7)
    rest = values - first
    second = lax.reduce_precision(rest, 8, 7)
    third = lax.reduce_precision(rest - second, 8, 7)
    return jnp.concatenate([first, second, third]).astype(BF)


def with_vectors(rows, *vectors):
    terms = jnp.concatenate([three_terms(vector) for vector in vectors]).reshape(-1, HD)
    padding = jnp.zeros((-terms.shape[0] % 16, HD), BF)
    return row_major(jnp.concatenate([rows, terms, padding], axis=0))


def whole(memory_space):
    return pl.BlockSpec(memory_space=memory_space)


def tile_of(rows, columns):
    return pl.BlockSpec((rows, columns), lambda i: (i, 0))


def group_mask(tile):
    return (tile >> 1) * CORE | (tile & 1) * LOW


def tile_column(document_ref, device):
    length = document_ref.shape[1]
    across = jnp.broadcast_to(document_ref[pl.ds(device, 1), :], (length, length))
    place_in = lax.broadcasted_iota(jnp.int32, (length, length), 0)
    return jnp.transpose(across), device * length + place_in


def hidden_bias(document_ref, column, device, masks, keys_across):
    documents, places = column
    length = document_ref.shape[1]
    parts = []
    for mask in masks:
        other = device ^ mask
        row = document_ref[pl.ds(other, 1), :]
        index = other * length + lax.broadcasted_iota(jnp.int32, (1, length), 1)
        ordered = index <= places if keys_across else index >= places
        parts.append(jnp.where((documents == row) & ordered, 0.0, MASKED))
    return jnp.concatenate(parts, axis=1)


def piece_masks(piece, pieces):
    blocks = pieces // 2
    return [(piece // blocks) * CORE | (piece % blocks) * BLOCK | z for z in range(4)]


def part_masks(piece, pieces):
    blocks = pieces // 2
    return [(piece // blocks) * HALF | (piece % blocks) * BLOCK | mask for mask in GROUP]


def attend(query_rot, keyval_pieces, documents, device):
    pieces, length = len(keyval_pieces), documents.shape[1]
    each = keyval_pieces[0].shape[0]

    def body(device_ref, document_ref, query_ref, *refs):
        piece_refs, (mixed_ref, log_ref, score_ref) = refs[:pieces], refs[pieces:]
        own = device_ref[0]
        column = tile_column(document_ref, own ^ group_mask(pl.program_id(0)))
        query = query_ref[...]
        row_max = jnp.full((length, 1), MASKED, F32)
        for p in range(pieces):
            bias = hidden_bias(document_ref, column, own, piece_masks(p, pieces), True)
            scores = contract_last(query, piece_refs[p][:, :HD]) + bias
            score_ref[:, p * each : (p + 1) * each] = scores
            row_max = jnp.maximum(row_max, jnp.max(scores, axis=1, keepdims=True))
        row_sum = jnp.zeros((length, 1), F32)
        total = jnp.zeros((length, HD), F32)
        for p in range(pieces):
            weights = jnp.exp(score_ref[:, p * each : (p + 1) * each] - row_max)
            row_sum = row_sum + jnp.sum(weights, axis=1, keepdims=True)
            total = total + dot(weights.astype(BF), piece_refs[p][:, HD:])
        mixed_ref[...] = (total / row_sum).astype(BF)
        log_ref[...] = row_max + jnp.log(row_sum)

    rows = query_rot.shape[0]
    return pl.pallas_call(
        body,
        grid=(rows // length,),
        out_shape=(
            jax.ShapeDtypeStruct((rows, HD), BF),
            jax.ShapeDtypeStruct((rows, 1), F32),
        ),
        in_specs=[whole(pltpu.SMEM), whole(pltpu.VMEM), tile_of(length, HD)]
        + [whole(pltpu.VMEM)] * pieces,
        out_specs=(tile_of(length, HD), tile_of(length, 1)),
        scratch_shapes=[pltpu.VMEM((length, pieces * each), F32)],
    )(device[None], documents, query_rot, *keyval_pieces)


def query_grads(query_rot, grad_mixed, mixed, log_norm, keyval_pieces, documents, device):
    pieces, length = len(keyval_pieces), documents.shape[1]

    def body(device_ref, document_ref, query_ref, grad_ref, mixed_ref, log_ref, *refs):
        piece_refs, out_ref = refs[:pieces], refs[pieces]
        own = device_ref[0]
        column = tile_column(document_ref, own ^ group_mask(pl.program_id(0)))
        query, grad, log = query_ref[...], grad_ref[...], log_ref[...]
        delta = jnp.sum(grad.astype(F32) * mixed_ref[...].astype(F32), axis=1, keepdims=True)
        total = jnp.zeros((length, HD), F32)
        for p in range(pieces):
            bias = hidden_bias(document_ref, column, own, piece_masks(p, pieces), True)
            keys = piece_refs[p][:, :HD]
            weights = jnp.exp(contract_last(query, keys) + bias - log)
            grad_prob = contract_last(grad, piece_refs[p][:, HD:])
            total = total + dot((weights * (grad_prob - delta)).astype(BF), keys)
        out_ref[...] = total

    rows = query_rot.shape[0]
    return pl.pallas_call(
        body,
        grid=(rows // length,),
        out_shape=jax.ShapeDtypeStruct((rows, HD), F32),
        in_specs=[whole(pltpu.SMEM), whole(pltpu.VMEM)]
        + [tile_of(length, HD)] * 3
        + [tile_of(length, 1)]
        + [whole(pltpu.VMEM)] * pieces,
        out_specs=tile_of(length, HD),
    )(device[None], documents, query_rot, grad_mixed, mixed, log_norm, *keyval_pieces)


def keyval_grads_of(keyval_group, part_query, part_grad, documents, device):
    pieces, length = len(part_query), documents.shape[1]
    each = part_query[0].shape[0]
    lines = each // HD

    def body(device_ref, document_ref, keyval_ref, *refs):
        query_refs, grad_refs, out_ref = refs[:pieces], refs[pieces : 2 * pieces], refs[-1]
        own = device_ref[0]
        column = tile_column(document_ref, own ^ group_mask(pl.program_id(0)))
        keys, values = keyval_ref[:, :HD], keyval_ref[:, HD:]
        grad_keys = jnp.zeros((length, HD), F32)
        grad_values = jnp.zeros((length, HD), F32)
        for p in range(pieces):
            bias = hidden_bias(document_ref, column, own, part_masks(p, pieces), False)
            terms = grad_refs[p][each:, :].astype(F32)

            def vector(first):
                sums = [
                    sum(terms[first + k * lines + j : first + k * lines + j + 1] for k in range(3))
                    for j in range(lines)
                ]
                return jnp.concatenate(sums, axis=1)

            queries, grads = query_refs[p][...], grad_refs[p][:each, :]
            weights = jnp.exp(contract_last(keys, queries) + bias - vector(0))
            grad_prob = contract_last(values, grads)
            grad_score = (weights * (grad_prob - vector(3 * lines))).astype(BF)
            grad_keys = grad_keys + dot(grad_score, queries)
            grad_values = grad_values + dot(weights.astype(BF), grads)
        out_ref[:, :HD] = grad_keys
        out_ref[:, HD:] = grad_values

    rows = keyval_group.shape[0]
    return pl.pallas_call(
        body,
        grid=(rows // length,),
        out_shape=jax.ShapeDtypeStruct((rows, 2 * HD), F32),
        in_specs=[whole(pltpu.SMEM), whole(pltpu.VMEM), tile_of(length, 2 * HD)]
        + [whole(pltpu.VMEM)] * (2 * pieces),
        out_specs=tile_of(length, 2 * HD),
    )(device[None], documents, keyval_group, *part_query, *part_grad)


def per_device(
    block_in,
    out_grad,
    segments,
    w_query,
    w_keyval,
    w_out,
    w_gate,
    w_up,
    w_down,
    gain_pre_attn,
    gain_post_attn,
    gain_pre_ffn,
    gain_post_ffn,
    gain_query,
    gain_key,
):
    devices = device_count()
    blocks = devices >> 3
    device = own_device()
    own_block, own_core, own_half, own_low = place(device)
    row_count, width = block_in.shape
    group_rows = row_count * len(GROUP)
    small_rows = w_keyval.shape[0]
    weight_rows = w_query.shape[0]
    big = gain_pre_attn.shape[0]
    little = gain_query.shape[0]
    per_owner = 4 * big + 2 * little

    gains_row, at = 0.0, 0
    for gain in (gain_pre_attn, gain_post_attn, gain_pre_ffn, gain_post_ffn, gain_query, gain_key):
        count = gain.shape[0]
        gains_row = gains_row + jnp.pad(gain.astype(F32), (at, 2 * HD - at - count))
        at = at + count
    below = 7 - small_rows % 8
    small = jnp.pad(w_keyval.astype(F32), ((0, 1 + below), (0, 0)))
    small = (small + jnp.pad(gains_row[None, :], ((small_rows, below), (0, 0)))).astype(BF)
    small = jnp.stack([small] + [flip(small, mask) for mask in (1, 2, 3)])
    near = jnp.stack([small] + [flip(small, mask) for mask in block_masks()[1:]])
    keyval_full, gains = shared_rows(near, flip(near, CORE), device, small_rows)
    gains = gains[:, :per_owner]
    scale_pre_attn = gains[:, :big].reshape(width)
    scale_post_attn = gains[:, big : 2 * big].reshape(width)
    scale_pre_ffn = gains[:, 2 * big : 3 * big].reshape(width)
    scale_post_ffn = gains[:, 3 * big : 4 * big].reshape(width)
    scale_query = gains[:, 4 * big : 4 * big + little].reshape(HD)
    scale_key = gains[:, 4 * big + little :].reshape(HD)
    head_weights = weight_pair(jnp.concatenate([w_query, w_out.T], axis=1), 0)
    head_weights = [head_weights] + [flip(head_weights, mask) for mask in block_masks()[1:]]
    gate_full = lax.all_gather(after(w_gate, near), "dp", axis=0, tiled=True)

    own_index = jnp.concatenate(
        [
            (device ^ mask) * row_count + jnp.arange(row_count, dtype=jnp.int32)
            for mask in GROUP
        ]
    )

    inv_in = rms_inverse(block_in)
    unit_in = block_in * inv_in
    unit_own = unit_in.astype(BF)
    unit_all = group_gather(unit_own)
    keyval = dot((unit_own.astype(F32) * scale_pre_attn).astype(BF), keyval_full)
    cosine, sine_part = rope_tables(own_index)
    key_proj = keyval[:, :HD]
    inv_key = rms_inverse(key_proj)
    key_rot = apply_rope(
        key_proj * inv_key * scale_key, cosine[:row_count], sine_part[:row_count]
    ).astype(BF)
    keyval_own = jnp.concatenate([key_rot, keyval[:, HD:].astype(BF)], axis=1)
    keyval_near, keyval_rest = token_gather(keyval_own)
    head_weights = [after(piece, keyval_own) for piece in head_weights]
    unit_all = after(unit_all, keyval_own)
    head_weights = natural(jnp.stack(head_weights), own_block).reshape(width, 2 * HD)
    query_full = head_weights[:, :HD]
    out_full = head_weights[:, HD:]
    gathered_in = (unit_all.astype(F32) * scale_pre_attn).astype(BF)
    queries = dot(gathered_in, query_full)
    inv_query = rms_inverse(queries)
    query_rot = (
        apply_rope(queries * inv_query * scale_query, cosine, sine_part) * QUERY_SCALE
    ).astype(BF)

    keyval_pieces = keyval_rest(query_rot)
    up_full = lax.all_gather(after(w_up, query_rot, *keyval_near), "dp", axis=0, tiled=True)
    down_full = lax.all_gather(after(w_down, query_rot, *keyval_near), "dp", axis=1, tiled=True)
    keyval_group = jnp.concatenate(
        [keyval_pieces[0][: 2 * row_count], keyval_pieces[blocks][: 2 * row_count]], axis=0
    )

    documents = segments.reshape(devices, row_count)
    mixed, log_norm = attend(query_rot, keyval_pieces, documents, device)
    attn_out = group_scatter(lambda rows: contract_last(rows, out_full), mixed)
    inv_attn = rms_inverse(attn_out)
    resid_mid = block_in + attn_out * inv_attn * scale_post_attn

    inv_mid = rms_inverse(resid_mid)
    normed_mid = (resid_mid * inv_mid * scale_pre_ffn).astype(BF)
    gathered_mid = column_gather(normed_mid)
    part_query = head_gather(after(query_rot, gathered_mid))
    gate_pre = dot(gathered_mid, gate_full)
    up_proj = dot(gathered_mid, up_full)
    gate_act, gate_deriv = gelu_pair(gate_pre)
    hidden = after((gate_act * up_proj).astype(BF), part_query[blocks])
    ffn_out = column_scatter(lambda rows: dot(rows, down_full), hidden)
    ffn_out = after(ffn_out, *part_query)
    inv_ffn = rms_inverse(ffn_out)
    block_out = resid_mid + ffn_out * inv_ffn * scale_post_ffn
    grad_ffn, grad_post_ffn = rms_backward(ffn_out, inv_ffn, scale_post_ffn, out_grad)
    grad_ffn_all = column_gather(grad_ffn.astype(BF))
    grad_w_down = column_major(contract_first(hidden, grad_ffn_all).astype(BF))
    grad_ffn_all = after(grad_ffn_all, grad_w_down)
    owned_down = lax.psum_scatter(grad_w_down, "dp", scatter_dimension=1, tiled=True)
    grad_hidden = contract_last(grad_ffn_all, down_full)
    grad_gate = (grad_hidden * up_proj * gate_deriv).astype(BF)
    grad_up = (grad_hidden * gate_act).astype(BF)
    grad_mid = column_scatter(
        lambda gate, up: contract_last(gate, gate_full) + contract_last(up, up_full),
        grad_gate,
        grad_up,
    )
    grad_w_gate = row_major(contract_first(gathered_mid, grad_gate).astype(BF))
    grad_w_up = row_major(contract_first(gathered_mid, grad_up).astype(BF))
    grad_mid = after(grad_mid, grad_w_gate)
    owned_gate = lax.psum_scatter(grad_w_gate, "dp", scatter_dimension=0, tiled=True)
    grad_resid, grad_pre_ffn = rms_backward(resid_mid, inv_mid, scale_pre_ffn, grad_mid)
    grad_resid_mid = out_grad + grad_resid

    grad_attn, grad_post_attn = rms_backward(attn_out, inv_attn, scale_post_attn, grad_resid_mid)
    grad_attn_all = group_gather(grad_attn.astype(BF))
    grad_attn_all = after(grad_attn_all, grad_w_up)
    owned_up = lax.psum_scatter(grad_w_up, "dp", scatter_dimension=0, tiled=True)
    grad_mixed = dot(grad_attn_all, out_full).astype(BF)
    delta = jnp.sum(grad_mixed.astype(F32) * mixed.astype(F32), axis=1)
    part_grad = head_gather(with_vectors(grad_mixed, log_norm[:, 0], delta))
    grad_w_out = contract_first(grad_attn_all, mixed)
    grad_query_rot = query_grads(
        query_rot, grad_mixed, mixed, log_norm, keyval_pieces, documents, device
    )
    owned_down = owned_down.astype(F32)
    part_grad = [after(part_grad[0], owned_down)] + part_grad[1:]
    grad_keyval_part = keyval_grads_of(keyval_group, part_query, part_grad, documents, device)
    grad_keyval_rows = group_scatter(lambda rows: rows, grad_keyval_part)

    grad_query_norm = rope_back(grad_query_rot, cosine, sine_part) * QUERY_SCALE
    grad_queries, grad_gain_query = rms_backward(queries, inv_query, scale_query, grad_query_norm)
    grad_query_bf = grad_queries.astype(BF)
    grad_w_query = contract_first(gathered_in, grad_query_bf)
    heads_pair = scatter_blocks(
        jnp.concatenate(
            [
                after(grad_w_query.astype(BF), *part_grad).reshape(blocks, 2, weight_rows, HD),
                grad_w_out.astype(BF).reshape(blocks, 2, weight_rows, HD),
            ],
            axis=2,
        ).reshape(blocks, 4 * weight_rows, HD)
    )
    grad_key_norm = rope_back(grad_keyval_rows[:, :HD], cosine[:row_count], sine_part[:row_count])
    grad_key_proj, grad_gain_key = rms_backward(key_proj, inv_key, scale_key, grad_key_norm)
    grad_keyval_bf = jnp.concatenate([grad_key_proj, grad_keyval_rows[:, HD:]], axis=1).astype(BF)
    keyval_grads_all = group_gather(grad_keyval_bf)
    heads_pair = after(heads_pair, keyval_grads_all)
    heads_owned = grad_owner(heads_pair.reshape(2, 2 * weight_rows, HD))
    owned_query, owned_out = heads_owned[:weight_rows], heads_owned[weight_rows:]
    grad_w_keyval = contract_first(gathered_in, keyval_grads_all)
    normed_query = contract_last(grad_query_bf, query_full)
    normed_keyval = contract_last(grad_keyval_bf, keyval_full)
    grad_pre_attn = jnp.sum(normed_query * unit_all.astype(F32), axis=0) + jnp.sum(
        normed_keyval * unit_in, axis=0
    )
    grad_normed = group_scatter(lambda rows: rows, normed_query) + normed_keyval
    grad_in_norm, _ = rms_backward(block_in, inv_in, scale_pre_attn, grad_normed)
    grad_in = grad_resid_mid + grad_in_norm

    gain_grads = jnp.concatenate(
        [
            g.reshape(devices, -1)
            for g in (
                grad_pre_attn,
                grad_post_attn,
                grad_pre_ffn,
                grad_post_ffn,
                grad_gain_query,
                grad_gain_key,
            )
        ],
        axis=1,
    ).reshape(blocks, 2, 2, 2, per_owner)

    def choose(array, index, axis):
        return lax.dynamic_index_in_dim(array, index, axis, keepdims=False)

    gain_sums = choose(gain_grads, own_core, 1) + flip(choose(gain_grads, 1 - own_core, 1), CORE)
    gain_sums = choose(gain_sums, own_low, 2) + flip(choose(gain_sums, 1 - own_low, 2), LOW)

    def two_rows(sums):
        high = lax.reduce_precision(sums, 8, 7)
        pair = jnp.stack([high, sums - high], axis=-2)
        pair = jnp.pad(pair, [(0, 0)] * (pair.ndim - 2) + [(0, 6), (0, HD - per_owner)])
        return pair

    keyval_grads = grad_w_keyval.astype(BF).reshape(blocks, 2, 2, 2, small_rows, 2 * HD)
    keyval_grads = choose(choose(keyval_grads, own_core, 1), own_low, 2)
    keyval_grads = jnp.concatenate(
        [keyval_grads[..., :HD], keyval_grads[..., HD:], two_rows(gain_sums).astype(BF)], axis=2
    )
    extra = keyval_grads.shape[2]
    others = scatter_blocks(keyval_grads.reshape(blocks, 2 * extra, HD)).reshape(2, extra, HD)
    mine, theirs = choose(others, own_half, 0), choose(others, 1 - own_half, 0)
    gains_at = 2 * small_rows
    theirs = jnp.concatenate(
        [theirs[:gains_at], two_rows(theirs[gains_at, :per_owner] + theirs[gains_at + 1, :per_owner])]
    )
    others = mine + flip(theirs.astype(BF), HALF).astype(F32)
    owned_keyval = jnp.concatenate([others[:small_rows], others[small_rows:gains_at]], axis=1)
    owned_up = after(owned_up, others).astype(F32)
    owned_gains = others[gains_at, :per_owner] + others[gains_at + 1, :per_owner]
    return (
        block_out,
        grad_in,
        owned_query,
        owned_keyval,
        owned_out.T,
        owned_gate.astype(F32),
        owned_up,
        owned_down,
        owned_gains[:big],
        owned_gains[big : 2 * big],
        owned_gains[2 * big : 3 * big],
        owned_gains[3 * big : 4 * big],
        owned_gains[4 * big : 4 * big + little],
        owned_gains[4 * big + little :],
    )


def solution(mesh):
    return jax.shard_map(
        per_device,
        mesh=mesh,
        in_specs=(
            P(("dp", "tensor"), None),
            P(("dp", "tensor"), None),
            P(),
            P("dp", "tensor"),
            P(("dp", "tensor"), None),
            P("tensor", "dp"),
            P("dp", "tensor"),
            P("dp", "tensor"),
            P("tensor", "dp"),
            P(("dp", "tensor")),
            P(("dp", "tensor")),
            P(("dp", "tensor")),
            P(("dp", "tensor")),
            P(("dp", "tensor")),
            P(("dp", "tensor")),
        ),
        out_specs=(
            P(("dp", "tensor"), None),
            P(("dp", "tensor"), None),
            P("dp", "tensor"),
            P(("dp", "tensor"), None),
            P("tensor", "dp"),
            P("dp", "tensor"),
            P("dp", "tensor"),
            P("tensor", "dp"),
            P(("dp", "tensor")),
            P(("dp", "tensor")),
            P(("dp", "tensor")),
            P(("dp", "tensor")),
            P(("dp", "tensor")),
            P(("dp", "tensor")),
        ),
        check_vma=False,
    )
```

```python
import jax
import jax.numpy as jnp
from jax import lax
from jax.experimental import pallas as pl
from jax.experimental.layout import Layout, with_layout_constraint
from jax.experimental.pallas import tpu as pltpu
from jax.sharding import PartitionSpec as P

HD = 256

EPSILON = 1e-06
ROPE_BASE = 1000000.0
QUERY_SCALE = 0.0625
MASKED = -1e30
GELU_COEF = 0.7978845608028654
GELU_CUBIC = 0.044715
BF = jnp.bfloat16
F32 = jnp.float32


def rms_inverse(values):
    return lax.rsqrt(jnp.mean(values * values, axis=-1, keepdims=True) + EPSILON)


def rms_backward(values, inverse, scales, upstream):
    weighted = upstream * scales
    inner_mean = jnp.mean(values * weighted, axis=-1, keepdims=True)
    grad_values = inverse * weighted - values * (inverse * inverse * inverse) * inner_mean
    grad_scales = jnp.sum(upstream * values * inverse, axis=0)
    return (grad_values, grad_scales)


def gelu_pair(values):
    inside = GELU_COEF * (values + GELU_CUBIC * values * values * values)
    tangent = jnp.tanh(inside)
    output = 0.5 * values * (1.0 + tangent)
    derivative = 0.5 * (1.0 + tangent) + 0.5 * values * (1.0 - tangent * tangent) * GELU_COEF * (
        1.0 + 3.0 * GELU_CUBIC * values * values
    )
    return (output, derivative)


def rotate_half(values):
    halfway = values.shape[-1] // 2
    return jnp.concatenate([-values[..., halfway:], values[..., :halfway]], axis=-1)


def rope_tables(positions):
    halfway = HD // 2
    frequency = ROPE_BASE ** (-2.0 * jnp.arange(halfway, dtype=F32) / HD)
    angles = positions.astype(F32)[:, None] * frequency[None, :]
    angles = jnp.concatenate([angles, angles], axis=1)
    return (jnp.cos(angles), jnp.sin(angles))


def apply_rope(values, cosine, sine_part):
    return values * cosine + rotate_half(values) * sine_part


def rope_back(upstream, cosine, sine_part):
    return upstream * cosine - rotate_half(upstream * sine_part)


def dot(left, right):
    return jnp.dot(left, right, preferred_element_type=F32)


def contract_first(left, right):
    return lax.dot_general(left, right, (((0,), (0,)), ((), ())), preferred_element_type=F32)


def contract_last(left, right):
    return lax.dot_general(left, right, (((1,), (1,)), ((), ())), preferred_element_type=F32)

AXES = ("dp", "tensor")
PAIR = 2


def place(device):
    return device >> 3, (device >> 2) & 1, (device >> 1) & 1, device & 1


def device_at(block, core, half, low):
    return (block << 3) | (core << 2) | (half << 1) | low


def device_count():
    return lax.axis_size("dp") * lax.axis_size("tensor")


def own_device():
    return lax.axis_index("dp") * lax.axis_size("tensor") + lax.axis_index("tensor")


def flip(value, mask):
    return lax.ppermute(value, AXES, [(s, s ^ mask) for s in range(device_count())])


def send(value, target):
    pairs = [(s, target(*place(s))) for s in range(device_count())]
    return lax.ppermute(value, AXES, [(s, t) for s, t in pairs if t is not None])


LOW, HALF, CORE, BLOCK = 1, 2, 4, 8
GROUP = (0, LOW, CORE, CORE | LOW)


def block_masks():
    return [BLOCK * k for k in range(lax.axis_size("dp") // PAIR)]


def natural(items, index):
    count, rows, columns = items.shape

    def body(index_ref, item_ref, out_ref):
        out_ref[...] = item_ref[...]

    return pl.pallas_call(
        body,
        out_shape=jax.ShapeDtypeStruct(items.shape, items.dtype),
        grid_spec=pltpu.PrefetchScalarGridSpec(
            num_scalar_prefetch=1,
            grid=(count,),
            in_specs=[pl.BlockSpec((1, rows, columns), lambda i, ref: (i ^ ref[0], 0, 0))],
            out_specs=pl.BlockSpec((1, rows, columns), lambda i, ref: (i, 0, 0)),
        ),
    )(index[None], items)


def shared_rows(near, far, device, rows):
    blocks, _, _, columns = near.shape
    count = 8 * blocks

    def body(index_ref, near_ref, far_ref, rows_ref, gains_ref, wide_ref):
        for owner in range(count):
            at = owner ^ index_ref[0]
            block, low = at >> 3, at & 3
            mine = near_ref[block, low].astype(F32)
            other = far_ref[block, low].astype(F32)
            piece = jnp.where((at & CORE) == 0, mine, other)
            wide_ref[owner * rows : (owner + 1) * rows, :] = piece[:rows]
            gains_ref[owner : owner + 1, :] = piece[rows : rows + 1]
        rows_ref[...] = wide_ref[...].astype(BF)

    return pl.pallas_call(
        body,
        out_shape=(
            jax.ShapeDtypeStruct((count * rows, columns), BF),
            jax.ShapeDtypeStruct((count, columns), F32),
        ),
        in_specs=[
            pl.BlockSpec(memory_space=pltpu.SMEM),
            pl.BlockSpec(memory_space=pltpu.VMEM),
            pl.BlockSpec(memory_space=pltpu.VMEM),
        ],
        out_specs=(
            pl.BlockSpec(memory_space=pltpu.VMEM),
            pl.BlockSpec(memory_space=pltpu.VMEM),
        ),
        scratch_shapes=[pltpu.VMEM((count * rows, columns), F32)],
    )(device[None], near, far)


def row_major(values):
    return with_layout_constraint(values, Layout(major_to_minor=(0, 1)))


def column_major(values):
    return with_layout_constraint(values, Layout(major_to_minor=(1, 0)))


def group_gather(values):
    near = flip(values, LOW)
    across = flip(values, CORE)
    return jnp.concatenate([values, near, across, flip(near, CORE)], axis=0)


def group_scatter(product, *rows):
    middle = rows[0].shape[0] // 2
    length = middle // 2
    far = flip(product(*[r[middle:] for r in rows]).astype(BF), CORE)
    near = product(*[r[:middle] for r in rows]) + far.astype(F32)
    return near[:length] + flip(near[length:].astype(BF), LOW).astype(F32)


def after(value, *others):
    return lax.optimization_barrier((value, *others))[0]


def column_gather(values):
    return jnp.concatenate([values] + [flip(values, mask) for mask in (1, 2, 3)], axis=0)


def column_scatter(product, *rows):
    middle = rows[0].shape[0] // 2
    length = middle // 2
    sent = product(*[r[middle:] for r in rows]).astype(BF)
    far = [flip(sent[length:], 3), flip(sent[:length], 2)]
    near = product(*[r[:middle] for r in rows])
    near = near[:length] + flip(near[length:].astype(BF), 1).astype(F32)
    return near + far[0].astype(F32) + far[1].astype(F32), sent


def exchange_first(value):
    def target(block, core, half, low):
        if half == core:
            return device_at(block, core, 1 - half, low)
        return device_at(block, 1 - core, half, low)

    return send(value, target)


def exchange_second(value):
    def target(block, core, half, low):
        return None if half == core else device_at(block, 1 - core, 1 - half, low)

    return send(value, target)


def weight_pair(value, axis):
    _, core, half, _ = place(own_device())
    first, second = exchange_first(value), exchange_second(value)
    kept = jnp.where(half == core, value, second)
    return jnp.concatenate(
        [jnp.where(half == 0, kept, first), jnp.where(half == 0, first, kept)], axis=axis
    )


def grad_owner(pair):
    return jnp.sum(jnp.stack(grad_owner_parts(pair)), axis=0)


def grad_owner_parts(pair):
    _, core, half, _ = place(own_device())
    pair = pair.astype(BF)
    first = jnp.where(half == 0, pair[1], pair[0])
    second = jnp.where(half == 0, pair[0], pair[1])
    got = exchange_second(second)
    return [
        exchange_first_back(first).astype(F32),
        jnp.where(half == core, second, got).astype(F32),
    ]


def exchange_first_back(value):
    def target(block, core, half, low):
        if half == core:
            return device_at(block, 1 - core, half, low)
        return device_at(block, core, 1 - half, low)

    return send(value, target)


def scatter_blocks(values):
    own = own_device() >> 3
    total = lax.dynamic_index_in_dim(values, own, 0, keepdims=False).astype(F32)
    for mask in block_masks()[1:]:
        piece = lax.dynamic_index_in_dim(values, own ^ (mask // BLOCK), 0, keepdims=False)
        total = total + flip(piece.astype(BF), mask).astype(F32)
    return total


def head_gather(values):
    near = [flip(values, mask) for mask in block_masks()[1:]]
    other = flip(values, HALF)
    far = [flip(other, mask) for mask in block_masks()[1:]]
    return [values, *near, other, *far]


def token_gather(values):
    column = jnp.concatenate([values] + [flip(values, mask) for mask in (1, 2, 3)], axis=0)
    near = [column] + [flip(column, mask) for mask in block_masks()[1:]]
    return near, lambda later: near + [flip(after(piece, later), CORE) for piece in near]


def three_terms(values):
    first = lax.reduce_precision(values, 8, 7)
    rest = values - first
    second = lax.reduce_precision(rest, 8, 7)
    third = lax.reduce_precision(rest - second, 8, 7)
    return jnp.concatenate([first, second, third]).astype(BF)


def with_vectors(rows, *vectors):
    terms = jnp.concatenate([three_terms(vector) for vector in vectors]).reshape(-1, HD)
    padding = jnp.zeros((-terms.shape[0] % 16, HD), BF)
    return row_major(jnp.concatenate([rows, terms, padding], axis=0))


def whole(memory_space):
    return pl.BlockSpec(memory_space=memory_space)


def tile_of(rows, columns):
    return pl.BlockSpec((rows, columns), lambda i: (i, 0))


def group_mask(tile):
    return (tile >> 1) * CORE | (tile & 1) * LOW


def tile_column(document_ref, device):
    length = document_ref.shape[1]
    across = jnp.broadcast_to(document_ref[pl.ds(device, 1), :], (length, length))
    place_in = lax.broadcasted_iota(jnp.int32, (length, length), 0)
    return jnp.transpose(across), device * length + place_in


def hidden_bias(document_ref, column, device, masks, keys_across):
    documents, places = column
    length = document_ref.shape[1]
    parts = []
    for mask in masks:
        other = device ^ mask
        row = document_ref[pl.ds(other, 1), :]
        index = other * length + lax.broadcasted_iota(jnp.int32, (1, length), 1)
        ordered = index <= places if keys_across else index >= places
        parts.append(jnp.where((documents == row) & ordered, 0.0, MASKED))
    return jnp.concatenate(parts, axis=1)


def piece_masks(piece, pieces):
    blocks = pieces // 2
    return [(piece // blocks) * CORE | (piece % blocks) * BLOCK | z for z in range(4)]


def part_masks(piece, pieces):
    blocks = pieces // 2
    return [(piece // blocks) * HALF | (piece % blocks) * BLOCK | mask for mask in GROUP]


def attend(query_rot, keyval_pieces, documents, device):
    pieces, length = len(keyval_pieces), documents.shape[1]
    each = keyval_pieces[0].shape[0]

    def body(device_ref, document_ref, query_ref, *refs):
        piece_refs, (mixed_ref, log_ref, score_ref) = refs[:pieces], refs[pieces:]
        own = device_ref[0]
        column = tile_column(document_ref, own ^ group_mask(pl.program_id(0)))
        query = query_ref[...]
        row_max = jnp.full((length, 1), MASKED, F32)
        for p in range(pieces):
            bias = hidden_bias(document_ref, column, own, piece_masks(p, pieces), True)
            scores = contract_last(query, piece_refs[p][:, :HD]) + bias
            score_ref[:, p * each : (p + 1) * each] = scores
            row_max = jnp.maximum(row_max, jnp.max(scores, axis=1, keepdims=True))
        row_sum = jnp.zeros((length, 1), F32)
        total = jnp.zeros((length, HD), F32)
        for p in range(pieces):
            weights = jnp.exp(score_ref[:, p * each : (p + 1) * each] - row_max)
            row_sum = row_sum + jnp.sum(weights, axis=1, keepdims=True)
            total = total + dot(weights.astype(BF), piece_refs[p][:, HD:])
        mixed_ref[...] = (total / row_sum).astype(BF)
        log_ref[...] = row_max + jnp.log(row_sum)

    rows = query_rot.shape[0]
    return pl.pallas_call(
        body,
        grid=(rows // length,),
        out_shape=(
            jax.ShapeDtypeStruct((rows, HD), BF),
            jax.ShapeDtypeStruct((rows, 1), F32),
        ),
        in_specs=[whole(pltpu.SMEM), whole(pltpu.VMEM), tile_of(length, HD)]
        + [whole(pltpu.VMEM)] * pieces,
        out_specs=(tile_of(length, HD), tile_of(length, 1)),
        scratch_shapes=[pltpu.VMEM((length, pieces * each), F32)],
    )(device[None], documents, query_rot, *keyval_pieces)


def query_grads(query_rot, grad_mixed, mixed, log_norm, keyval_pieces, documents, device):
    pieces, length = len(keyval_pieces), documents.shape[1]

    def body(device_ref, document_ref, query_ref, grad_ref, mixed_ref, log_ref, *refs):
        piece_refs, out_ref = refs[:pieces], refs[pieces]
        own = device_ref[0]
        column = tile_column(document_ref, own ^ group_mask(pl.program_id(0)))
        query, grad, log = query_ref[...], grad_ref[...], log_ref[...]
        delta = jnp.sum(grad.astype(F32) * mixed_ref[...].astype(F32), axis=1, keepdims=True)
        total = jnp.zeros((length, HD), F32)
        for p in range(pieces):
            bias = hidden_bias(document_ref, column, own, piece_masks(p, pieces), True)
            keys = piece_refs[p][:, :HD]
            weights = jnp.exp(contract_last(query, keys) + bias - log)
            grad_prob = contract_last(grad, piece_refs[p][:, HD:])
            total = total + dot((weights * (grad_prob - delta)).astype(BF), keys)
        out_ref[...] = total

    rows = query_rot.shape[0]
    return pl.pallas_call(
        body,
        grid=(rows // length,),
        out_shape=jax.ShapeDtypeStruct((rows, HD), F32),
        in_specs=[whole(pltpu.SMEM), whole(pltpu.VMEM)]
        + [tile_of(length, HD)] * 3
        + [tile_of(length, 1)]
        + [whole(pltpu.VMEM)] * pieces,
        out_specs=tile_of(length, HD),
    )(device[None], documents, query_rot, grad_mixed, mixed, log_norm, *keyval_pieces)


def keyval_grads_of(keyval_group, part_query, part_grad, documents, device):
    pieces, length = len(part_query), documents.shape[1]
    each = part_query[0].shape[0]
    lines = each // HD

    def body(device_ref, document_ref, keyval_ref, *refs):
        query_refs, grad_refs, out_ref = refs[:pieces], refs[pieces : 2 * pieces], refs[-1]
        own = device_ref[0]
        column = tile_column(document_ref, own ^ group_mask(pl.program_id(0)))
        keys, values = keyval_ref[:, :HD], keyval_ref[:, HD:]
        grad_keys = jnp.zeros((length, HD), F32)
        grad_values = jnp.zeros((length, HD), F32)
        for p in range(pieces):
            bias = hidden_bias(document_ref, column, own, part_masks(p, pieces), False)
            terms = grad_refs[p][each:, :].astype(F32)

            def vector(first):
                sums = [
                    sum(terms[first + k * lines + j : first + k * lines + j + 1] for k in range(3))
                    for j in range(lines)
                ]
                return jnp.concatenate(sums, axis=1)

            queries, grads = query_refs[p][...], grad_refs[p][:each, :]
            weights = jnp.exp(contract_last(keys, queries) + bias - vector(0))
            grad_prob = contract_last(values, grads)
            grad_score = (weights * (grad_prob - vector(3 * lines))).astype(BF)
            grad_keys = grad_keys + dot(grad_score, queries)
            grad_values = grad_values + dot(weights.astype(BF), grads)
        out_ref[:, :HD] = grad_keys
        out_ref[:, HD:] = grad_values

    rows = keyval_group.shape[0]
    return pl.pallas_call(
        body,
        grid=(rows // length,),
        out_shape=jax.ShapeDtypeStruct((rows, 2 * HD), F32),
        in_specs=[whole(pltpu.SMEM), whole(pltpu.VMEM), tile_of(length, 2 * HD)]
        + [whole(pltpu.VMEM)] * (2 * pieces),
        out_specs=tile_of(length, 2 * HD),
    )(device[None], documents, keyval_group, *part_query, *part_grad)


def per_device(
    block_in,
    out_grad,
    segments,
    w_query,
    w_keyval,
    w_out,
    w_gate,
    w_up,
    w_down,
    gain_pre_attn,
    gain_post_attn,
    gain_pre_ffn,
    gain_post_ffn,
    gain_query,
    gain_key,
):
    devices = device_count()
    blocks = devices >> 3
    device = own_device()
    own_block, own_core, own_half, own_low = place(device)
    row_count, width = block_in.shape
    group_rows = row_count * len(GROUP)
    small_rows = w_keyval.shape[0]
    weight_rows = w_query.shape[0]
    big = gain_pre_attn.shape[0]
    little = gain_query.shape[0]
    per_owner = 4 * big + 2 * little

    gains_row, at = 0.0, 0
    for gain in (gain_pre_attn, gain_post_attn, gain_pre_ffn, gain_post_ffn, gain_query, gain_key):
        count = gain.shape[0]
        gains_row = gains_row + jnp.pad(gain.astype(F32), (at, 2 * HD - at - count))
        at = at + count
    below = 7 - small_rows % 8
    small = jnp.pad(w_keyval.astype(F32), ((0, 1 + below), (0, 0)))
    small = (small + jnp.pad(gains_row[None, :], ((small_rows, below), (0, 0)))).astype(BF)
    small = jnp.stack([small] + [flip(small, mask) for mask in (1, 2, 3)])
    near = jnp.stack([small] + [flip(small, mask) for mask in block_masks()[1:]])
    keyval_full, gains = shared_rows(near, flip(near, CORE), device, small_rows)
    gains = gains[:, :per_owner]
    scale_pre_attn = gains[:, :big].reshape(width)
    scale_post_attn = gains[:, big : 2 * big].reshape(width)
    scale_pre_ffn = gains[:, 2 * big : 3 * big].reshape(width)
    scale_post_ffn = gains[:, 3 * big : 4 * big].reshape(width)
    scale_query = gains[:, 4 * big : 4 * big + little].reshape(HD)
    scale_key = gains[:, 4 * big + little :].reshape(HD)
    head_weights = weight_pair(jnp.concatenate([w_query, w_out.T], axis=1), 0)
    head_weights = [head_weights] + [flip(head_weights, mask) for mask in block_masks()[1:]]
    gate_full = lax.all_gather(after(w_gate, near), "dp", axis=0, tiled=True)

    own_index = jnp.concatenate(
        [
            (device ^ mask) * row_count + jnp.arange(row_count, dtype=jnp.int32)
            for mask in GROUP
        ]
    )

    inv_in = rms_inverse(block_in)
    unit_in = block_in * inv_in
    unit_own = unit_in.astype(BF)
    unit_all = group_gather(unit_own)
    keyval = dot((unit_own.astype(F32) * scale_pre_attn).astype(BF), keyval_full)
    cosine, sine_part = rope_tables(own_index)
    key_proj = keyval[:, :HD]
    inv_key = rms_inverse(key_proj)
    key_rot = apply_rope(
        key_proj * inv_key * scale_key, cosine[:row_count], sine_part[:row_count]
    ).astype(BF)
    keyval_own = jnp.concatenate([key_rot, keyval[:, HD:].astype(BF)], axis=1)
    keyval_near, keyval_rest = token_gather(keyval_own)
    head_weights = [after(piece, keyval_own) for piece in head_weights]
    unit_all = after(unit_all, keyval_own)
    head_weights = natural(jnp.stack(head_weights), own_block).reshape(width, 2 * HD)
    query_full = head_weights[:, :HD]
    out_full = head_weights[:, HD:]
    gathered_in = (unit_all.astype(F32) * scale_pre_attn).astype(BF)
    queries = dot(gathered_in, query_full)
    inv_query = rms_inverse(queries)
    query_rot = (
        apply_rope(queries * inv_query * scale_query, cosine, sine_part) * QUERY_SCALE
    ).astype(BF)

    keyval_pieces = keyval_rest(query_rot)
    up_full = lax.all_gather(after(w_up, query_rot, *keyval_near), "dp", axis=0, tiled=True)
    down_full = lax.all_gather(after(w_down, query_rot, *keyval_near), "dp", axis=1, tiled=True)
    keyval_group = jnp.concatenate(
        [keyval_pieces[0][: 2 * row_count], keyval_pieces[blocks][: 2 * row_count]], axis=0
    )

    documents = segments.reshape(devices, row_count)
    mixed, log_norm = attend(query_rot, keyval_pieces, documents, device)
    attn_out = group_scatter(lambda rows: contract_last(rows, out_full), mixed)
    inv_attn = rms_inverse(attn_out)
    resid_mid = block_in + attn_out * inv_attn * scale_post_attn

    inv_mid = rms_inverse(resid_mid)
    normed_mid = (resid_mid * inv_mid * scale_pre_ffn).astype(BF)
    gathered_mid = column_gather(normed_mid)
    part_query = head_gather(after(query_rot, gathered_mid))
    gate_pre = dot(gathered_mid, gate_full)
    up_proj = dot(gathered_mid, up_full)
    gate_act, gate_deriv = gelu_pair(gate_pre)
    hidden = after((gate_act * up_proj).astype(BF), part_query[blocks])
    ffn_out, _ = column_scatter(lambda rows: dot(rows, down_full), hidden)
    ffn_out = after(ffn_out, *part_query[: blocks + 1])
    inv_ffn = rms_inverse(ffn_out)
    block_out = resid_mid + ffn_out * inv_ffn * scale_post_ffn
    grad_ffn, grad_post_ffn = rms_backward(ffn_out, inv_ffn, scale_post_ffn, out_grad)
    grad_ffn_all = after(column_gather(grad_ffn.astype(BF)), *part_query)
    grad_w_down = column_major(contract_first(hidden, grad_ffn_all).astype(BF))
    grad_ffn_all = after(grad_ffn_all, grad_w_down)
    owned_down = lax.psum_scatter(grad_w_down, "dp", scatter_dimension=1, tiled=True)
    grad_hidden = contract_last(grad_ffn_all, down_full)
    grad_gate = (grad_hidden * up_proj * gate_deriv).astype(BF)
    grad_up = (grad_hidden * gate_act).astype(BF)
    grad_mid, grad_mid_sent = column_scatter(
        lambda gate, up: contract_last(gate, gate_full) + contract_last(up, up_full),
        grad_gate,
        grad_up,
    )
    mid_later = after(gathered_mid, grad_mid_sent)
    grad_w_gate = row_major(contract_first(mid_later, grad_gate).astype(BF))
    grad_w_up = row_major(contract_first(mid_later, grad_up).astype(BF))
    grad_mid = after(grad_mid, grad_w_gate, grad_w_up)
    owned_gate = lax.psum_scatter(grad_w_gate, "dp", scatter_dimension=0, tiled=True)
    grad_resid, grad_pre_ffn = rms_backward(resid_mid, inv_mid, scale_pre_ffn, grad_mid)
    grad_resid_mid = out_grad + grad_resid

    grad_attn, grad_post_attn = rms_backward(attn_out, inv_attn, scale_post_attn, grad_resid_mid)
    grad_attn_all = group_gather(grad_attn.astype(BF))
    owned_up = lax.psum_scatter(grad_w_up, "dp", scatter_dimension=0, tiled=True)
    grad_mixed = dot(grad_attn_all, out_full).astype(BF)
    delta = jnp.sum(grad_mixed.astype(F32) * mixed.astype(F32), axis=1)
    part_grad = head_gather(with_vectors(grad_mixed, log_norm[:, 0], delta))
    grad_w_out = contract_first(grad_attn_all, mixed)
    grad_query_rot = query_grads(
        query_rot, grad_mixed, mixed, log_norm, keyval_pieces, documents, device
    )
    owned_down = owned_down.astype(F32)
    part_grad = [after(part_grad[0], owned_down)] + part_grad[1:]
    grad_keyval_part = keyval_grads_of(keyval_group, part_query, part_grad, documents, device)
    grad_query_norm = rope_back(grad_query_rot, cosine, sine_part) * QUERY_SCALE
    grad_queries, grad_gain_query = rms_backward(queries, inv_query, scale_query, grad_query_norm)
    grad_query_bf = grad_queries.astype(BF)
    grad_w_query = contract_first(gathered_in, grad_query_bf)
    heads_pair = scatter_blocks(
        jnp.concatenate(
            [
                after(grad_w_query.astype(BF), *part_grad).reshape(blocks, 2, weight_rows, HD),
                grad_w_out.astype(BF).reshape(blocks, 2, weight_rows, HD),
            ],
            axis=2,
        ).reshape(blocks, 4 * weight_rows, HD)
    )
    grad_keyval_part = after(grad_keyval_part, heads_pair)
    grad_keyval_rows = group_scatter(lambda rows: rows, grad_keyval_part)

    grad_key_norm = rope_back(grad_keyval_rows[:, :HD], cosine[:row_count], sine_part[:row_count])
    grad_key_proj, grad_gain_key = rms_backward(key_proj, inv_key, scale_key, grad_key_norm)
    grad_keyval_bf = jnp.concatenate([grad_key_proj, grad_keyval_rows[:, HD:]], axis=1).astype(BF)
    keyval_grads_all = group_gather(grad_keyval_bf)
    heads_pair = after(heads_pair, keyval_grads_all)
    heads_owned = grad_owner(heads_pair.reshape(2, 2 * weight_rows, HD))
    owned_query, owned_out = heads_owned[:weight_rows], heads_owned[weight_rows:]
    grad_w_keyval = contract_first(gathered_in, keyval_grads_all)
    normed_query = contract_last(grad_query_bf, query_full)
    normed_keyval = contract_last(grad_keyval_bf, keyval_full)
    grad_pre_attn = jnp.sum(normed_query * unit_all.astype(F32), axis=0) + jnp.sum(
        normed_keyval * unit_in, axis=0
    )
    grad_normed = group_scatter(lambda rows: rows, normed_query) + normed_keyval
    grad_in_norm, _ = rms_backward(block_in, inv_in, scale_pre_attn, grad_normed)
    grad_in = grad_resid_mid + grad_in_norm

    gain_grads = jnp.concatenate(
        [
            g.reshape(devices, -1)
            for g in (
                grad_pre_attn,
                grad_post_attn,
                grad_pre_ffn,
                grad_post_ffn,
                grad_gain_query,
                grad_gain_key,
            )
        ],
        axis=1,
    ).reshape(blocks, 2, 2, 2, per_owner)

    def choose(array, index, axis):
        return lax.dynamic_index_in_dim(array, index, axis, keepdims=False)

    gain_sums = choose(gain_grads, own_core, 1) + flip(choose(gain_grads, 1 - own_core, 1), CORE)
    gain_sums = choose(gain_sums, own_low, 2) + flip(choose(gain_sums, 1 - own_low, 2), LOW)

    def two_rows(sums):
        high = lax.reduce_precision(sums, 8, 7)
        pair = jnp.stack([high, sums - high], axis=-2)
        pair = jnp.pad(pair, [(0, 0)] * (pair.ndim - 2) + [(0, 6), (0, HD - per_owner)])
        return pair

    keyval_grads = grad_w_keyval.astype(BF).reshape(blocks, 2, 2, 2, small_rows, 2 * HD)
    keyval_grads = choose(choose(keyval_grads, own_core, 1), own_low, 2)
    keyval_grads = jnp.concatenate(
        [keyval_grads[..., :HD], keyval_grads[..., HD:], two_rows(gain_sums).astype(BF)], axis=2
    )
    extra = keyval_grads.shape[2]
    others = scatter_blocks(keyval_grads.reshape(blocks, 2 * extra, HD)).reshape(2, extra, HD)
    mine, theirs = choose(others, own_half, 0), choose(others, 1 - own_half, 0)
    gains_at = 2 * small_rows
    theirs = jnp.concatenate(
        [theirs[:gains_at], two_rows(theirs[gains_at, :per_owner] + theirs[gains_at + 1, :per_owner])]
    )
    others = mine + flip(theirs.astype(BF), HALF).astype(F32)
    owned_keyval = jnp.concatenate([others[:small_rows], others[small_rows:gains_at]], axis=1)
    owned_up = after(owned_up, others).astype(F32)
    owned_gains = others[gains_at, :per_owner] + others[gains_at + 1, :per_owner]
    return (
        block_out,
        grad_in,
        owned_query,
        owned_keyval,
        owned_out.T,
        owned_gate.astype(F32),
        owned_up,
        owned_down,
        owned_gains[:big],
        owned_gains[big : 2 * big],
        owned_gains[2 * big : 3 * big],
        owned_gains[3 * big : 4 * big],
        owned_gains[4 * big : 4 * big + little],
        owned_gains[4 * big + little :],
    )


def solution(mesh):
    return jax.shard_map(
        per_device,
        mesh=mesh,
        in_specs=(
            P(("dp", "tensor"), None),
            P(("dp", "tensor"), None),
            P(),
            P("dp", "tensor"),
            P(("dp", "tensor"), None),
            P("tensor", "dp"),
            P("dp", "tensor"),
            P("dp", "tensor"),
            P("tensor", "dp"),
            P(("dp", "tensor")),
            P(("dp", "tensor")),
            P(("dp", "tensor")),
            P(("dp", "tensor")),
            P(("dp", "tensor")),
            P(("dp", "tensor")),
        ),
        out_specs=(
            P(("dp", "tensor"), None),
            P(("dp", "tensor"), None),
            P("dp", "tensor"),
            P(("dp", "tensor"), None),
            P("tensor", "dp"),
            P("dp", "tensor"),
            P("dp", "tensor"),
            P("tensor", "dp"),
            P(("dp", "tensor")),
            P(("dp", "tensor")),
            P(("dp", "tensor")),
            P(("dp", "tensor")),
            P(("dp", "tensor")),
            P(("dp", "tensor")),
        ),
        check_vma=False,
    )
```

```python
import jax
import jax.numpy as jnp
from jax import lax
from jax.experimental import pallas as pl
from jax.experimental.layout import Layout, with_layout_constraint
from jax.experimental.pallas import tpu as pltpu
from jax.sharding import PartitionSpec as P

HD = 256

EPSILON = 1e-06
ROPE_BASE = 1000000.0
QUERY_SCALE = 0.0625
MASKED = -1e30
GELU_COEF = 0.7978845608028654
GELU_CUBIC = 0.044715
BF = jnp.bfloat16
F32 = jnp.float32


def rms_inverse(values):
    return lax.rsqrt(jnp.mean(values * values, axis=-1, keepdims=True) + EPSILON)


def rms_backward(values, inverse, scales, upstream):
    weighted = upstream * scales
    inner_mean = jnp.mean(values * weighted, axis=-1, keepdims=True)
    grad_values = inverse * weighted - values * (inverse * inverse * inverse) * inner_mean
    grad_scales = jnp.sum(upstream * values * inverse, axis=0)
    return (grad_values, grad_scales)


def gelu_pair(values):
    inside = GELU_COEF * (values + GELU_CUBIC * values * values * values)
    tangent = jnp.tanh(inside)
    output = 0.5 * values * (1.0 + tangent)
    derivative = 0.5 * (1.0 + tangent) + 0.5 * values * (1.0 - tangent * tangent) * GELU_COEF * (
        1.0 + 3.0 * GELU_CUBIC * values * values
    )
    return (output, derivative)


def rotate_half(values):
    halfway = values.shape[-1] // 2
    return jnp.concatenate([-values[..., halfway:], values[..., :halfway]], axis=-1)


def rope_tables(positions):
    halfway = HD // 2
    frequency = ROPE_BASE ** (-2.0 * jnp.arange(halfway, dtype=F32) / HD)
    angles = positions.astype(F32)[:, None] * frequency[None, :]
    angles = jnp.concatenate([angles, angles], axis=1)
    return (jnp.cos(angles), jnp.sin(angles))


def apply_rope(values, cosine, sine_part):
    return values * cosine + rotate_half(values) * sine_part


def rope_back(upstream, cosine, sine_part):
    return upstream * cosine - rotate_half(upstream * sine_part)


def dot(left, right):
    return jnp.dot(left, right, preferred_element_type=F32)


def contract_first(left, right):
    return lax.dot_general(left, right, (((0,), (0,)), ((), ())), preferred_element_type=F32)


def contract_last(left, right):
    return lax.dot_general(left, right, (((1,), (1,)), ((), ())), preferred_element_type=F32)

AXES = ("dp", "tensor")
PAIR = 2


def place(device):
    return device >> 3, (device >> 2) & 1, (device >> 1) & 1, device & 1


def device_at(block, core, half, low):
    return (block << 3) | (core << 2) | (half << 1) | low


def device_count():
    return lax.axis_size("dp") * lax.axis_size("tensor")


def own_device():
    return lax.axis_index("dp") * lax.axis_size("tensor") + lax.axis_index("tensor")


def flip(value, mask):
    return lax.ppermute(value, AXES, [(s, s ^ mask) for s in range(device_count())])


def send(value, target):
    pairs = [(s, target(*place(s))) for s in range(device_count())]
    return lax.ppermute(value, AXES, [(s, t) for s, t in pairs if t is not None])


LOW, HALF, CORE, BLOCK = 1, 2, 4, 8
GROUP = (0, LOW, CORE, CORE | LOW)


def block_masks():
    return [BLOCK * k for k in range(lax.axis_size("dp") // PAIR)]


def natural(items, index):
    count, rows, columns = items.shape

    def body(index_ref, item_ref, out_ref):
        out_ref[...] = item_ref[...]

    return pl.pallas_call(
        body,
        out_shape=jax.ShapeDtypeStruct(items.shape, items.dtype),
        grid_spec=pltpu.PrefetchScalarGridSpec(
            num_scalar_prefetch=1,
            grid=(count,),
            in_specs=[pl.BlockSpec((1, rows, columns), lambda i, ref: (i ^ ref[0], 0, 0))],
            out_specs=pl.BlockSpec((1, rows, columns), lambda i, ref: (i, 0, 0)),
        ),
    )(index[None], items)


def shared_rows(near, far, device, rows):
    blocks, _, _, columns = near.shape
    count = 8 * blocks

    def body(index_ref, near_ref, far_ref, rows_ref, gains_ref, wide_ref):
        for owner in range(count):
            at = owner ^ index_ref[0]
            block, low = at >> 3, at & 3
            mine = near_ref[block, low].astype(F32)
            other = far_ref[block, low].astype(F32)
            piece = jnp.where((at & CORE) == 0, mine, other)
            wide_ref[owner * rows : (owner + 1) * rows, :] = piece[:rows]
            gains_ref[owner : owner + 1, :] = piece[rows : rows + 1]
        rows_ref[...] = wide_ref[...].astype(BF)

    return pl.pallas_call(
        body,
        out_shape=(
            jax.ShapeDtypeStruct((count * rows, columns), BF),
            jax.ShapeDtypeStruct((count, columns), F32),
        ),
        in_specs=[
            pl.BlockSpec(memory_space=pltpu.SMEM),
            pl.BlockSpec(memory_space=pltpu.VMEM),
            pl.BlockSpec(memory_space=pltpu.VMEM),
        ],
        out_specs=(
            pl.BlockSpec(memory_space=pltpu.VMEM),
            pl.BlockSpec(memory_space=pltpu.VMEM),
        ),
        scratch_shapes=[pltpu.VMEM((count * rows, columns), F32)],
    )(device[None], near, far)


def row_major(values):
    return with_layout_constraint(values, Layout(major_to_minor=(0, 1)))


def column_major(values):
    return with_layout_constraint(values, Layout(major_to_minor=(1, 0)))


def group_gather(values):
    near = flip(values, LOW)
    across = flip(values, CORE)
    return jnp.concatenate([values, near, across, flip(near, CORE)], axis=0)


def group_scatter(product, *rows):
    middle = rows[0].shape[0] // 2
    length = middle // 2
    far = flip(product(*[r[middle:] for r in rows]).astype(BF), CORE)
    near = product(*[r[:middle] for r in rows]) + far.astype(F32)
    return near[:length] + flip(near[length:].astype(BF), LOW).astype(F32)


def after(value, *others):
    return lax.optimization_barrier((value, *others))[0]


def column_gather(values):
    return jnp.concatenate([values] + [flip(values, mask) for mask in (1, 2, 3)], axis=0)


def column_scatter(product, *rows):
    middle = rows[0].shape[0] // 2
    length = middle // 2
    sent = product(*[r[middle:] for r in rows]).astype(BF)
    far = [flip(sent[length:], 3), flip(sent[:length], 2)]
    near = product(*[r[:middle] for r in rows])
    near = near[:length] + flip(near[length:].astype(BF), 1).astype(F32)
    return near + far[0].astype(F32) + far[1].astype(F32), sent


def exchange_first(value):
    def target(block, core, half, low):
        if half == core:
            return device_at(block, core, 1 - half, low)
        return device_at(block, 1 - core, half, low)

    return send(value, target)


def exchange_second(value):
    def target(block, core, half, low):
        return None if half == core else device_at(block, 1 - core, 1 - half, low)

    return send(value, target)


def weight_pair(value, axis):
    _, core, half, _ = place(own_device())
    first, second = exchange_first(value), exchange_second(value)
    kept = jnp.where(half == core, value, second)
    return jnp.concatenate(
        [jnp.where(half == 0, kept, first), jnp.where(half == 0, first, kept)], axis=axis
    )


def grad_owner(pair):
    return jnp.sum(jnp.stack(grad_owner_parts(pair)), axis=0)


def grad_owner_parts(pair):
    _, core, half, _ = place(own_device())
    pair = pair.astype(BF)
    first = jnp.where(half == 0, pair[1], pair[0])
    second = jnp.where(half == 0, pair[0], pair[1])
    got = exchange_second(second)
    return [
        exchange_first_back(first).astype(F32),
        jnp.where(half == core, second, got).astype(F32),
    ]


def exchange_first_back(value):
    def target(block, core, half, low):
        if half == core:
            return device_at(block, 1 - core, half, low)
        return device_at(block, core, 1 - half, low)

    return send(value, target)


def scatter_blocks(values):
    own = own_device() >> 3
    total = lax.dynamic_index_in_dim(values, own, 0, keepdims=False).astype(F32)
    for mask in block_masks()[1:]:
        piece = lax.dynamic_index_in_dim(values, own ^ (mask // BLOCK), 0, keepdims=False)
        total = total + flip(piece.astype(BF), mask).astype(F32)
    return total


def head_gather(values):
    near = [flip(values, mask) for mask in block_masks()[1:]]
    other = flip(values, HALF)
    far = [flip(other, mask) for mask in block_masks()[1:]]
    return [values, *near, other, *far]


def token_gather(values):
    column = jnp.concatenate([values] + [flip(values, mask) for mask in (1, 2, 3)], axis=0)
    near = [column] + [flip(column, mask) for mask in block_masks()[1:]]
    return near, lambda later: near + [flip(after(piece, later), CORE) for piece in near]


def three_terms(values):
    first = lax.reduce_precision(values, 8, 7)
    rest = values - first
    second = lax.reduce_precision(rest, 8, 7)
    third = lax.reduce_precision(rest - second, 8, 7)
    return jnp.concatenate([first, second, third]).astype(BF)


def with_vectors(rows, *vectors):
    terms = jnp.concatenate([three_terms(vector) for vector in vectors]).reshape(-1, HD)
    padding = jnp.zeros((-terms.shape[0] % 16, HD), BF)
    return row_major(jnp.concatenate([rows, terms, padding], axis=0))


def whole(memory_space):
    return pl.BlockSpec(memory_space=memory_space)


def tile_of(rows, columns):
    return pl.BlockSpec((rows, columns), lambda i: (i, 0))


def group_mask(tile):
    return (tile >> 1) * CORE | (tile & 1) * LOW


def tile_column(document_ref, device):
    length = document_ref.shape[1]
    across = jnp.broadcast_to(document_ref[pl.ds(device, 1), :], (length, length))
    place_in = lax.broadcasted_iota(jnp.int32, (length, length), 0)
    return jnp.transpose(across), device * length + place_in


def hidden_bias(document_ref, column, device, masks, keys_across):
    documents, places = column
    length = document_ref.shape[1]
    parts = []
    for mask in masks:
        other = device ^ mask
        row = document_ref[pl.ds(other, 1), :]
        index = other * length + lax.broadcasted_iota(jnp.int32, (1, length), 1)
        ordered = index <= places if keys_across else index >= places
        parts.append(jnp.where((documents == row) & ordered, 0.0, MASKED))
    return jnp.concatenate(parts, axis=1)


def piece_masks(piece, pieces):
    blocks = pieces // 2
    return [(piece // blocks) * CORE | (piece % blocks) * BLOCK | z for z in range(4)]


def part_masks(piece, pieces):
    blocks = pieces // 2
    return [(piece // blocks) * HALF | (piece % blocks) * BLOCK | mask for mask in GROUP]


def attend(query_rot, keyval_pieces, documents, device):
    pieces, length = len(keyval_pieces), documents.shape[1]
    each = keyval_pieces[0].shape[0]

    def body(device_ref, document_ref, query_ref, *refs):
        piece_refs, (mixed_ref, log_ref, score_ref) = refs[:pieces], refs[pieces:]
        own = device_ref[0]
        column = tile_column(document_ref, own ^ group_mask(pl.program_id(0)))
        query = query_ref[...]
        row_max = jnp.full((length, 1), MASKED, F32)
        for p in range(pieces):
            bias = hidden_bias(document_ref, column, own, piece_masks(p, pieces), True)
            scores = contract_last(query, piece_refs[p][:, :HD]) + bias
            score_ref[:, p * each : (p + 1) * each] = scores
            row_max = jnp.maximum(row_max, jnp.max(scores, axis=1, keepdims=True))
        row_sum = jnp.zeros((length, 1), F32)
        total = jnp.zeros((length, HD), F32)
        for p in range(pieces):
            weights = jnp.exp(score_ref[:, p * each : (p + 1) * each] - row_max)
            row_sum = row_sum + jnp.sum(weights, axis=1, keepdims=True)
            total = total + dot(weights.astype(BF), piece_refs[p][:, HD:])
        mixed_ref[...] = (total / row_sum).astype(BF)
        log_ref[...] = row_max + jnp.log(row_sum)

    rows = query_rot.shape[0]
    return pl.pallas_call(
        body,
        grid=(rows // length,),
        out_shape=(
            jax.ShapeDtypeStruct((rows, HD), BF),
            jax.ShapeDtypeStruct((rows, 1), F32),
        ),
        in_specs=[whole(pltpu.SMEM), whole(pltpu.VMEM), tile_of(length, HD)]
        + [whole(pltpu.VMEM)] * pieces,
        out_specs=(tile_of(length, HD), tile_of(length, 1)),
        scratch_shapes=[pltpu.VMEM((length, pieces * each), F32)],
    )(device[None], documents, query_rot, *keyval_pieces)


def query_grads(query_rot, grad_mixed, mixed, log_norm, keyval_pieces, documents, device):
    pieces, length = len(keyval_pieces), documents.shape[1]

    def body(device_ref, document_ref, query_ref, grad_ref, mixed_ref, log_ref, *refs):
        piece_refs, out_ref = refs[:pieces], refs[pieces]
        own = device_ref[0]
        column = tile_column(document_ref, own ^ group_mask(pl.program_id(0)))
        query, grad, log = query_ref[...], grad_ref[...], log_ref[...]
        delta = jnp.sum(grad.astype(F32) * mixed_ref[...].astype(F32), axis=1, keepdims=True)
        total = jnp.zeros((length, HD), F32)
        for p in range(pieces):
            bias = hidden_bias(document_ref, column, own, piece_masks(p, pieces), True)
            keys = piece_refs[p][:, :HD]
            weights = jnp.exp(contract_last(query, keys) + bias - log)
            grad_prob = contract_last(grad, piece_refs[p][:, HD:])
            total = total + dot((weights * (grad_prob - delta)).astype(BF), keys)
        out_ref[...] = total

    rows = query_rot.shape[0]
    return pl.pallas_call(
        body,
        grid=(rows // length,),
        out_shape=jax.ShapeDtypeStruct((rows, HD), F32),
        in_specs=[whole(pltpu.SMEM), whole(pltpu.VMEM)]
        + [tile_of(length, HD)] * 3
        + [tile_of(length, 1)]
        + [whole(pltpu.VMEM)] * pieces,
        out_specs=tile_of(length, HD),
    )(device[None], documents, query_rot, grad_mixed, mixed, log_norm, *keyval_pieces)


def keyval_grads_of(keyval_group, part_query, part_grad, documents, device):
    pieces, length = len(part_query), documents.shape[1]
    each = part_query[0].shape[0]
    lines = each // HD

    def body(device_ref, document_ref, keyval_ref, *refs):
        query_refs, grad_refs, out_ref = refs[:pieces], refs[pieces : 2 * pieces], refs[-1]
        own = device_ref[0]
        column = tile_column(document_ref, own ^ group_mask(pl.program_id(0)))
        keys, values = keyval_ref[:, :HD], keyval_ref[:, HD:]
        grad_keys = jnp.zeros((length, HD), F32)
        grad_values = jnp.zeros((length, HD), F32)
        for p in range(pieces):
            bias = hidden_bias(document_ref, column, own, part_masks(p, pieces), False)
            terms = grad_refs[p][each:, :].astype(F32)

            def vector(first):
                sums = [
                    sum(terms[first + k * lines + j : first + k * lines + j + 1] for k in range(3))
                    for j in range(lines)
                ]
                return jnp.concatenate(sums, axis=1)

            queries, grads = query_refs[p][...], grad_refs[p][:each, :]
            weights = jnp.exp(contract_last(keys, queries) + bias - vector(0))
            grad_prob = contract_last(values, grads)
            grad_score = (weights * (grad_prob - vector(3 * lines))).astype(BF)
            grad_keys = grad_keys + dot(grad_score, queries)
            grad_values = grad_values + dot(weights.astype(BF), grads)
        out_ref[:, :HD] = grad_keys
        out_ref[:, HD:] = grad_values

    rows = keyval_group.shape[0]
    return pl.pallas_call(
        body,
        grid=(rows // length,),
        out_shape=jax.ShapeDtypeStruct((rows, 2 * HD), F32),
        in_specs=[whole(pltpu.SMEM), whole(pltpu.VMEM), tile_of(length, 2 * HD)]
        + [whole(pltpu.VMEM)] * (2 * pieces),
        out_specs=tile_of(length, 2 * HD),
    )(device[None], documents, keyval_group, *part_query, *part_grad)


def per_device(
    block_in,
    out_grad,
    segments,
    w_query,
    w_keyval,
    w_out,
    w_gate,
    w_up,
    w_down,
    gain_pre_attn,
    gain_post_attn,
    gain_pre_ffn,
    gain_post_ffn,
    gain_query,
    gain_key,
):
    devices = device_count()
    blocks = devices >> 3
    device = own_device()
    own_block, own_core, own_half, own_low = place(device)
    row_count, width = block_in.shape
    group_rows = row_count * len(GROUP)
    small_rows = w_keyval.shape[0]
    weight_rows = w_query.shape[0]
    big = gain_pre_attn.shape[0]
    little = gain_query.shape[0]
    per_owner = 4 * big + 2 * little

    gains_row, at = 0.0, 0
    for gain in (gain_pre_attn, gain_post_attn, gain_pre_ffn, gain_post_ffn, gain_query, gain_key):
        count = gain.shape[0]
        gains_row = gains_row + jnp.pad(gain.astype(F32), (at, 2 * HD - at - count))
        at = at + count
    below = 7 - small_rows % 8
    small = jnp.pad(w_keyval.astype(F32), ((0, 1 + below), (0, 0)))
    small = (small + jnp.pad(gains_row[None, :], ((small_rows, below), (0, 0)))).astype(BF)
    small = jnp.stack([small] + [flip(small, mask) for mask in (1, 2, 3)])
    near = jnp.stack([small] + [flip(small, mask) for mask in block_masks()[1:]])
    keyval_full, gains = shared_rows(near, flip(near, CORE), device, small_rows)
    gains = gains[:, :per_owner]
    scale_pre_attn = gains[:, :big].reshape(width)
    scale_post_attn = gains[:, big : 2 * big].reshape(width)
    scale_pre_ffn = gains[:, 2 * big : 3 * big].reshape(width)
    scale_post_ffn = gains[:, 3 * big : 4 * big].reshape(width)
    scale_query = gains[:, 4 * big : 4 * big + little].reshape(HD)
    scale_key = gains[:, 4 * big + little :].reshape(HD)
    head_weights = weight_pair(jnp.concatenate([w_query, w_out.T], axis=1), 0)
    head_weights = after(head_weights, keyval_full)
    head_weights = [head_weights] + [flip(head_weights, mask) for mask in block_masks()[1:]]
    gate_full = lax.all_gather(after(w_gate, near), "dp", axis=0, tiled=True)

    own_index = jnp.concatenate(
        [
            (device ^ mask) * row_count + jnp.arange(row_count, dtype=jnp.int32)
            for mask in GROUP
        ]
    )

    inv_in = rms_inverse(block_in)
    unit_in = block_in * inv_in
    unit_own = unit_in.astype(BF)
    unit_all = group_gather(after(unit_own, keyval_full))
    keyval = dot((unit_own.astype(F32) * scale_pre_attn).astype(BF), keyval_full)
    cosine, sine_part = rope_tables(own_index)
    key_proj = keyval[:, :HD]
    inv_key = rms_inverse(key_proj)
    key_rot = apply_rope(
        key_proj * inv_key * scale_key, cosine[:row_count], sine_part[:row_count]
    ).astype(BF)
    keyval_own = jnp.concatenate([key_rot, keyval[:, HD:].astype(BF)], axis=1)
    keyval_near, keyval_rest = token_gather(keyval_own)
    head_weights = [after(piece, keyval_own) for piece in head_weights]
    unit_all = after(unit_all, keyval_own)
    head_weights = natural(jnp.stack(head_weights), own_block).reshape(width, 2 * HD)
    query_full = head_weights[:, :HD]
    out_full = head_weights[:, HD:]
    gathered_in = (unit_all.astype(F32) * scale_pre_attn).astype(BF)
    queries = dot(gathered_in, query_full)
    inv_query = rms_inverse(queries)
    query_rot = (
        apply_rope(queries * inv_query * scale_query, cosine, sine_part) * QUERY_SCALE
    ).astype(BF)

    keyval_pieces = keyval_rest(query_rot)
    up_full = lax.all_gather(after(w_up, query_rot, *keyval_near), "dp", axis=0, tiled=True)
    down_full = lax.all_gather(after(w_down, query_rot, *keyval_near), "dp", axis=1, tiled=True)
    keyval_group = jnp.concatenate(
        [keyval_pieces[0][: 2 * row_count], keyval_pieces[blocks][: 2 * row_count]], axis=0
    )

    documents = segments.reshape(devices, row_count)
    mixed, log_norm = attend(query_rot, keyval_pieces, documents, device)
    attn_out = group_scatter(lambda rows: contract_last(rows, out_full), mixed)
    inv_attn = rms_inverse(attn_out)
    resid_mid = block_in + attn_out * inv_attn * scale_post_attn

    inv_mid = rms_inverse(resid_mid)
    normed_mid = (resid_mid * inv_mid * scale_pre_ffn).astype(BF)
    gathered_mid = column_gather(normed_mid)
    part_query = head_gather(after(query_rot, gathered_mid))
    gate_pre = dot(gathered_mid, gate_full)
    up_proj = dot(gathered_mid, up_full)
    gate_act, gate_deriv = gelu_pair(gate_pre)
    hidden = after((gate_act * up_proj).astype(BF), part_query[blocks])
    ffn_out, _ = column_scatter(lambda rows: dot(rows, down_full), hidden)
    ffn_out = after(ffn_out, *part_query[: blocks + 1])
    inv_ffn = rms_inverse(ffn_out)
    block_out = resid_mid + ffn_out * inv_ffn * scale_post_ffn
    grad_ffn, grad_post_ffn = rms_backward(ffn_out, inv_ffn, scale_post_ffn, out_grad)
    grad_ffn_all = after(column_gather(grad_ffn.astype(BF)), *part_query)
    grad_w_down = column_major(contract_first(hidden, grad_ffn_all).astype(BF))
    grad_ffn_all = after(grad_ffn_all, grad_w_down)
    owned_down = lax.psum_scatter(grad_w_down, "dp", scatter_dimension=1, tiled=True)
    grad_hidden = contract_last(grad_ffn_all, down_full)
    grad_gate = (grad_hidden * up_proj * gate_deriv).astype(BF)
    grad_up = (grad_hidden * gate_act).astype(BF)
    grad_mid, grad_mid_sent = column_scatter(
        lambda gate, up: contract_last(gate, gate_full) + contract_last(up, up_full),
        grad_gate,
        grad_up,
    )
    mid_later = after(gathered_mid, grad_mid_sent)
    grad_w_gate = row_major(contract_first(mid_later, grad_gate).astype(BF))
    grad_w_up = row_major(contract_first(mid_later, grad_up).astype(BF))
    grad_mid = after(grad_mid, grad_w_gate, grad_w_up)
    owned_gate = lax.psum_scatter(grad_w_gate, "dp", scatter_dimension=0, tiled=True)
    grad_resid, grad_pre_ffn = rms_backward(resid_mid, inv_mid, scale_pre_ffn, grad_mid)
    grad_resid_mid = out_grad + grad_resid

    grad_attn, grad_post_attn = rms_backward(attn_out, inv_attn, scale_post_attn, grad_resid_mid)
    grad_attn_all = group_gather(grad_attn.astype(BF))
    owned_up = lax.psum_scatter(grad_w_up, "dp", scatter_dimension=0, tiled=True)
    grad_mixed = dot(grad_attn_all, out_full).astype(BF)
    delta = jnp.sum(grad_mixed.astype(F32) * mixed.astype(F32), axis=1)
    part_grad = head_gather(with_vectors(grad_mixed, log_norm[:, 0], delta))
    grad_w_out = contract_first(grad_attn_all, mixed)
    grad_query_rot = query_grads(
        query_rot, grad_mixed, mixed, log_norm, keyval_pieces, documents, device
    )
    owned_down = owned_down.astype(F32)
    part_grad = [after(part_grad[0], owned_down)] + part_grad[1:]
    grad_keyval_part = keyval_grads_of(keyval_group, part_query, part_grad, documents, device)
    grad_query_norm = rope_back(grad_query_rot, cosine, sine_part) * QUERY_SCALE
    grad_queries, grad_gain_query = rms_backward(queries, inv_query, scale_query, grad_query_norm)
    grad_query_bf = grad_queries.astype(BF)
    grad_w_query = contract_first(gathered_in, grad_query_bf)
    heads_pair = scatter_blocks(
        jnp.concatenate(
            [
                after(grad_w_query.astype(BF), *part_grad).reshape(blocks, 2, weight_rows, HD),
                grad_w_out.astype(BF).reshape(blocks, 2, weight_rows, HD),
            ],
            axis=2,
        ).reshape(blocks, 4 * weight_rows, HD)
    )
    grad_keyval_part = after(grad_keyval_part, heads_pair)
    grad_keyval_rows = group_scatter(lambda rows: rows, grad_keyval_part)

    grad_key_norm = rope_back(grad_keyval_rows[:, :HD], cosine[:row_count], sine_part[:row_count])
    grad_key_proj, grad_gain_key = rms_backward(key_proj, inv_key, scale_key, grad_key_norm)
    grad_keyval_bf = jnp.concatenate([grad_key_proj, grad_keyval_rows[:, HD:]], axis=1).astype(BF)
    keyval_grads_all = group_gather(grad_keyval_bf)
    heads_pair = after(heads_pair, keyval_grads_all)
    heads_owned = grad_owner(heads_pair.reshape(2, 2 * weight_rows, HD))
    owned_query, owned_out = heads_owned[:weight_rows], heads_owned[weight_rows:]
    grad_w_keyval = contract_first(gathered_in, keyval_grads_all)
    normed_query = contract_last(grad_query_bf, query_full)
    normed_keyval = contract_last(grad_keyval_bf, keyval_full)
    grad_pre_attn = jnp.sum(normed_query * unit_all.astype(F32), axis=0) + jnp.sum(
        normed_keyval * unit_in, axis=0
    )
    grad_normed = group_scatter(lambda rows: rows, normed_query) + normed_keyval
    grad_in_norm, _ = rms_backward(block_in, inv_in, scale_pre_attn, grad_normed)
    grad_in = grad_resid_mid + grad_in_norm

    gain_grads = jnp.concatenate(
        [
            g.reshape(devices, -1)
            for g in (
                grad_pre_attn,
                grad_post_attn,
                grad_pre_ffn,
                grad_post_ffn,
                grad_gain_query,
                grad_gain_key,
            )
        ],
        axis=1,
    ).reshape(blocks, 2, 2, 2, per_owner)

    def choose(array, index, axis):
        return lax.dynamic_index_in_dim(array, index, axis, keepdims=False)

    gain_sums = choose(gain_grads, own_core, 1) + flip(choose(gain_grads, 1 - own_core, 1), CORE)
    gain_sums = choose(gain_sums, own_low, 2) + flip(choose(gain_sums, 1 - own_low, 2), LOW)

    def two_rows(sums):
        high = lax.reduce_precision(sums, 8, 7)
        pair = jnp.stack([high, sums - high], axis=-2)
        pair = jnp.pad(pair, [(0, 0)] * (pair.ndim - 2) + [(0, 6), (0, HD - per_owner)])
        return pair

    keyval_grads = grad_w_keyval.astype(BF).reshape(blocks, 2, 2, 2, small_rows, 2 * HD)
    keyval_grads = choose(choose(keyval_grads, own_core, 1), own_low, 2)
    keyval_grads = jnp.concatenate(
        [keyval_grads[..., :HD], keyval_grads[..., HD:], two_rows(gain_sums).astype(BF)], axis=2
    )
    extra = keyval_grads.shape[2]
    others = scatter_blocks(keyval_grads.reshape(blocks, 2 * extra, HD)).reshape(2, extra, HD)
    mine, theirs = choose(others, own_half, 0), choose(others, 1 - own_half, 0)
    gains_at = 2 * small_rows
    theirs = jnp.concatenate(
        [theirs[:gains_at], two_rows(theirs[gains_at, :per_owner] + theirs[gains_at + 1, :per_owner])]
    )
    others = mine + flip(theirs.astype(BF), HALF).astype(F32)
    owned_keyval = jnp.concatenate([others[:small_rows], others[small_rows:gains_at]], axis=1)
    owned_up = after(owned_up, others).astype(F32)
    owned_gains = others[gains_at, :per_owner] + others[gains_at + 1, :per_owner]
    return (
        block_out,
        grad_in,
        owned_query,
        owned_keyval,
        owned_out.T,
        owned_gate.astype(F32),
        owned_up,
        owned_down,
        owned_gains[:big],
        owned_gains[big : 2 * big],
        owned_gains[2 * big : 3 * big],
        owned_gains[3 * big : 4 * big],
        owned_gains[4 * big : 4 * big + little],
        owned_gains[4 * big + little :],
    )


def solution(mesh):
    return jax.shard_map(
        per_device,
        mesh=mesh,
        in_specs=(
            P(("dp", "tensor"), None),
            P(("dp", "tensor"), None),
            P(),
            P("dp", "tensor"),
            P(("dp", "tensor"), None),
            P("tensor", "dp"),
            P("dp", "tensor"),
            P("dp", "tensor"),
            P("tensor", "dp"),
            P(("dp", "tensor")),
            P(("dp", "tensor")),
            P(("dp", "tensor")),
            P(("dp", "tensor")),
            P(("dp", "tensor")),
            P(("dp", "tensor")),
        ),
        out_specs=(
            P(("dp", "tensor"), None),
            P(("dp", "tensor"), None),
            P("dp", "tensor"),
            P(("dp", "tensor"), None),
            P("tensor", "dp"),
            P("dp", "tensor"),
            P("dp", "tensor"),
            P("tensor", "dp"),
            P(("dp", "tensor")),
            P(("dp", "tensor")),
            P(("dp", "tensor")),
            P(("dp", "tensor")),
            P(("dp", "tensor")),
            P(("dp", "tensor")),
        ),
        check_vma=False,
    )
```
